32 devices in a mesh: grp: 2 (over x), wave: 16 (over z, y, core).
Axes of the slice: x: 2, y: 2, z: 4, core: 2. Of those that a mesh axis runs over, the one named last changes fastest.
Arguments:
- spectral: bfloat16 [640, 641, 256], P(('grp', 'wave')), parts along dimension 0, may hold values from -0.23925781 to 0.23925781
- legendre: bfloat16 [320, 641, 320], P('wave'), may hold values from -0.25 to 0.25
- pair_low: int32 [320], replicated, may hold values from 0 to 319, each once
- routes: int32 [102400, 1], P(('grp', 'wave')), parts along dimension 0, may hold values from 0 to 15; in each aligned block of 3200 rows (0 to 3199, 3200 to 6399, ...) at most 400 rows name the same one
- w_in: bfloat16 [16, 128, 1024], P('wave'), may hold values from -0.5 to 0.5
- w_mid: bfloat16 [16, 1024, 1024], P('wave'), may hold values from -0.1875 to 0.1875
- w_out: bfloat16 [16, 1024, 128], P('wave'), may hold values from -1.5 to 1.5
Outputs:
- tendency: bfloat16 [640, 641, 256], P(('grp', 'wave')), parts along dimension 0
The draws below stay inside these ranges and needn't reach their ends.
There are 2 independent parts, one for each index of `grp`. The reference program is written for one: setup_inputs(seed, part) draws one part's arguments, and reference() takes and returns one part's arrays. A program takes and returns all parts, laid end to end along the dimension named above; an argument that names none is the same for every part. Nothing has to cross between parts.
Inputs may be any that keep to these rules, and one draw needn't show every extreme that they name: `routes`: among the columns of one device (each aligned block of 3200 columns) at most 400 name the same network, a bound that some block reaches of them.
All inputs are finite; a program needn't handle non-finite values.
Results may differ from the reference program's by a relative error of at most 0.01.
Values may be sent and summed in bfloat16 or wider, within the bound.
A program may use at most 192 MiB of HBM per device.

```python
import math
import jax
import jax.numpy as jnp
import numpy as np
from jax import lax

M = 640
LAT = 320
NLON = 1280
FIELDS = 4
HID = 1024
PAIRS = 320
J = 641
FL = 128
C = 256
COLUMNS = 51200
COLS_DEV = 3200
EXPERTS = 16
CAP = 400
N_WAVE = 16


def block_levels(own_key, dims, cuts, least, top_value):
    gain, own = 1.0, jax.random.fold_in(own_key, 6)
    for axis_at, parts in cuts:
        draws = jnp.exp(jax.random.uniform(jax.random.fold_in(own, axis_at), (parts,), jnp.float32, least / len(cuts), top_value / len(cuts)))
        gain = gain * jnp.repeat(draws, dims[axis_at] // parts).reshape([-1 if axis == axis_at else 1 for axis in range(len(dims))])
    return gain


def assign_block(rng, own, number, rows, number_of, top, reach, lean):
    order = jax.random.permutation(rng, number_of)
    packed, ordinary = shares(number_of, rows * top, reach, lean, True), shares(number_of, rows * top, reach, lean, False)
    places = jnp.arange(number_of)

    def named(sizes, rotation):
        used = int((sizes > 0).sum())
        fixed = max(1, used // 4)
        passed = fixed + (places - fixed + rotation * (used - fixed)) % max(1, number_of - fixed)
        return jnp.zeros((number_of,), jnp.int32).at[order[jnp.where(places < fixed, places, passed)]].set(jnp.asarray(sizes, jnp.int32))

    sizes = jnp.where(number % 4 == 0, named(packed, number // 4), named(ordinary, number - number // 4 - 1))
    mixed = jax.random.permutation(jax.random.fold_in(own, 3), number_of)
    giver, taker = mixed[0:number_of // 2 * 2:2], mixed[1:number_of // 2 * 2:2]
    slack = jnp.minimum(sizes[giver] - 1, reach - sizes[taker]) // 2
    slack = jnp.where((giver == order[0]) | (taker == order[0]) | (sizes[taker] == 0), 0, jnp.maximum(slack, 0))
    passed = jax.random.randint(jax.random.fold_in(own, 4), (number_of // 2,), 0, 1 << 20) % (slack + 1)
    sizes = sizes.at[giver].add(-passed).at[taker].add(passed)
    items = jnp.searchsorted(jnp.cumsum(sizes), jnp.arange(rows * top), side="right").astype(jnp.int32)
    listing = items.reshape(top, rows).T
    listing = listing[jax.random.permutation(jax.random.fold_in(own, 1), rows)]
    rotation = jax.random.randint(jax.random.fold_in(own, 2), (rows, 1), 0, top)
    return jnp.take_along_axis(listing, (jnp.arange(top)[None, :] + rotation) % top, axis=1)


def shares(count, total, limit, slope, full):
    portions = [(1 << 20) // math.isqrt(grade ** slope) + 1 for grade in range(1, count + 1)]
    largest = limit if full else min(limit, max(-(-total // count), total * portions[0] // sum(portions)))
    least = 1 if total - largest >= count - 1 else 0
    counts, surplus = [largest] + [least] * (count - 1), total - largest - least * (count - 1)
    while surplus > 0:
        free = [i for i in range(1, count) if counts[i] < largest] or [i for i in range(1, count) if counts[i] < limit]
        whole, remaining = sum([portions[i] for i in free]), surplus
        for i in free:
            more = min(limit - counts[i], max(1, remaining * portions[i] // whole), surplus)
            counts[i] = counts[i] + more
            surplus = surplus - more
    return np.array(counts)


def bell_draw(rng, shape, width, limit, shards=(), held_as=jnp.bfloat16):
    entries = jax.random.normal(rng, shape, jnp.float32) * width
    if len(shards) > 0:
        entries = block_levels(rng, shape, shards, -0.22, 0.18) * entries
    return jnp.clip(entries, min=-limit, max=limit).astype(held_as)


def setup_inputs(seed: int = 0, part: int = 0) -> dict:
    keys = jax.random.split(jax.random.key(seed), 8)
    part_splits = jax.random.split(jax.random.fold_in(keys[7], part), 8)
    spectral = bell_draw(part_splits[0], (PAIRS, J, C), 0.04, 0.23925781, ((0, 16),))
    legendre = bell_draw(keys[1], (PAIRS, J, LAT), J ** -0.5, 0.25, ((0, 16),))
    pair_low = jax.random.permutation(keys[2], PAIRS).astype(jnp.int32)
    routes_keys = jax.random.split(jax.random.fold_in(part_splits[3], 1), COLUMNS // COLS_DEV)
    routes_turns = jax.random.permutation(jax.random.fold_in(part_splits[3], 3), COLUMNS // COLS_DEV)
    routes = jax.vmap(lambda own, number: assign_block(jax.random.fold_in(part_splits[3], 2), own, number, COLS_DEV, EXPERTS, 1, CAP, 2))(routes_keys, routes_turns).reshape((COLUMNS, 1))
    w_in = bell_draw(keys[4], (EXPERTS, FL, HID), FL ** -0.5, 0.5, ((0, 16),))
    w_mid = bell_draw(keys[5], (EXPERTS, HID, HID), HID ** -0.5, 0.1875, ((0, 16),))
    w_out = bell_draw(keys[6], (EXPERTS, HID, FL), 0.25, 1.5, ((0, 16),))
    return dict(spectral=spectral, legendre=legendre, pair_low=pair_low, routes=routes, w_in=w_in, w_mid=w_mid, w_out=w_out)


def slot_waves(pair_low, wave_total):
    lower_wave = pair_low.astype(jnp.int32)
    return jnp.stack([lower_wave, wave_total - 1 - lower_wave], axis=1).reshape(-1)

def side_masks(pair_low, wave_total):
    degree = jnp.arange(wave_total + 1, dtype=jnp.int32)
    lower_side = degree[None, :] < (wave_total - pair_low.astype(jnp.int32))[:, None]
    return jnp.stack([lower_side, jnp.logical_not(lower_side)], axis=1)

def fourier_table(wavenums, points, inverse):
    longitude = jnp.arange(points, dtype=jnp.int32)
    phases = wavenums[:, None] * longitude[None, :] % points
    angles = phases.astype(jnp.float32) * jnp.float32(2.0 * math.pi / points)
    if inverse:
        factor = jnp.where(wavenums == 0, jnp.float32(1.0), jnp.float32(2.0))[:, None]
    else:
        factor = jnp.full((wavenums.shape[0], 1), 1.0 / math.sqrt(points), jnp.float32)
    return jnp.stack([factor * jnp.cos(angles), -factor * jnp.sin(angles)], axis=1).astype(jnp.bfloat16)

def forcing(grid_fields):
    flattened = grid_fields.reshape(FIELDS, -1)
    return (flattened * jnp.roll(flattened, -1, axis=0)).reshape(grid_fields.shape)

def coarse_columns(grid_fields):
    feat_width = grid_fields.shape[0]
    lat_rows = grid_fields.shape[1]
    lon_count = grid_fields.shape[2]
    blocks = grid_fields.reshape(feat_width, lat_rows // 2, 2, lon_count // 4, 4).mean(axis=(2, 4))
    return blocks.reshape(feat_width, -1).T.astype(jnp.bfloat16)

def spread_back(values, lat_rows):
    feat_width = values.shape[1]
    coarse = values.astype(jnp.float32).T.reshape(feat_width, lat_rows // 2, -1)
    before = jnp.roll(coarse, 1, axis=2)
    following = jnp.roll(coarse, -1, axis=2)
    pieces = [0.375 * before + 0.625 * coarse, 0.125 * before + 0.875 * coarse, 0.875 * coarse + 0.125 * following, 0.625 * coarse + 0.375 * following]
    fine_grid = jnp.stack(pieces, axis=3).reshape(feat_width, lat_rows // 2, -1)
    return jnp.repeat(fine_grid, 2, axis=1)

def slot_positions(regimes, experts_total):
    onehot = (regimes[:, :, None] == jnp.arange(experts_total, dtype=jnp.int32)).astype(jnp.int32)
    ranking = jnp.cumsum(onehot, axis=1) - 1
    return lax.optimization_barrier(jnp.sum(ranking * onehot, axis=2))

def network(columns, weight_in, weight_mid, weight_out):
    hidden = jax.nn.silu(jnp.dot(columns, weight_in, preferred_element_type=jnp.float32)).astype(jnp.bfloat16)
    deeper = jax.nn.silu(jnp.dot(hidden, weight_mid, preferred_element_type=jnp.float32)).astype(jnp.bfloat16)
    return jnp.dot(deeper, weight_out, preferred_element_type=jnp.float32).astype(jnp.bfloat16)

def reference(spectral, legendre, pair_low, routes, w_in, w_mid, w_out):
    pair_count = spectral.shape[0]
    degrees = spectral.shape[1]
    channels = spectral.shape[2]
    feat_width = channels // 2
    side_mask = side_masks(pair_low, M)

    def inverse_pair(bundle):
        coeffs, pair_table, side_rows = bundle
        masked = jnp.where(side_rows[:, :, None], coeffs.astype(jnp.float32)[None], 0.0)
        return jnp.einsum('sjc,jl->scl', masked, pair_table.astype(jnp.float32)).astype(jnp.bfloat16)
    fourier_in = lax.map(inverse_pair, (spectral, legendre, side_mask))
    fourier_in = fourier_in.reshape(2 * pair_count, feat_width, 2, LAT)
    wavenums = slot_waves(pair_low, M)
    inverse_table = fourier_table(wavenums, NLON, True)
    grid_fields = jnp.einsum('qfra,qrl->fal', fourier_in.astype(jnp.float32), inverse_table.astype(jnp.float32))
    forced = forcing(grid_fields)
    columns = coarse_columns(grid_fields)
    regimes = routes[:, 0].astype(jnp.int32).reshape(N_WAVE, COLS_DEV)
    positions = slot_positions(regimes, EXPERTS)
    sources = jnp.broadcast_to(jnp.arange(N_WAVE, dtype=jnp.int32)[:, None], regimes.shape)
    regime_flat = regimes.reshape(-1)
    source_flat = sources.reshape(-1)
    position_flat = positions.reshape(-1)
    buffer = jnp.zeros((EXPERTS, N_WAVE, CAP, feat_width), jnp.bfloat16)
    buffer = buffer.at[regime_flat, source_flat, position_flat].set(columns)

    def run_expert(bundle):
        block_rows, weight_in, weight_mid, weight_out = bundle
        return network(block_rows.reshape(-1, feat_width), weight_in, weight_mid, weight_out).reshape(block_rows.shape)
    results = lax.map(run_expert, (buffer, w_in, w_mid, w_out))
    returned = results[regime_flat, source_flat, position_flat]
    correction = spread_back(returned, LAT)
    tendency_grid = (forced + correction).astype(jnp.bfloat16)
    forward_table = fourier_table(wavenums, NLON, False)
    fourier_out = jnp.einsum('fal,qrl->qfra', tendency_grid.astype(jnp.float32), forward_table.astype(jnp.float32)).astype(jnp.bfloat16)
    fourier_out = fourier_out.reshape(pair_count, 2, feat_width, 2, LAT)

    def forward_pair(bundle):
        pair_table, coeffs, side_rows = bundle
        both_sides = jnp.einsum('jl,skrl->sjkr', pair_table.astype(jnp.float32), coeffs.astype(jnp.float32))
        summed = lax.optimization_barrier(jnp.sum(jnp.where(side_rows[:, :, None, None], both_sides, 0.0), axis=0))
        return summed.reshape(degrees, channels).astype(jnp.bfloat16)
    return lax.map(forward_pair, (legendre, fourier_out, side_mask))
```

```python
import functools
import math

import jax
import jax.numpy as jnp
from jax import lax
from jax.experimental import pallas as pl
from jax.experimental.pallas import tpu as pltpu
from jax.sharding import PartitionSpec as P

NLON = 1280
FIELDS = 4
PAIR_STEP = 4
ROW_PARTS = 5
SLOT_PARTS = 2


def slot_waves(pair_low, wave_total):
    return jnp.stack([pair_low, wave_total - 1 - pair_low], axis=1).reshape(-1)


def side_masks(pair_low, wave_total):
    degree = jnp.arange(wave_total + 1, dtype=jnp.int32)
    lower_side = degree[None, :] < (wave_total - pair_low)[:, None]
    return jnp.stack([lower_side, jnp.logical_not(lower_side)], axis=1)


def fourier_table(wavenums, points, inverse):
    longitude = jnp.arange(points, dtype=jnp.int32)
    phases = wavenums[:, None] * longitude[None, :] % points
    angles = phases.astype(jnp.float32) * jnp.float32(2.0 * math.pi / points)
    if inverse:
        factor = jnp.where(wavenums == 0, jnp.float32(1.0), jnp.float32(2.0))[:, None]
    else:
        factor = jnp.full((wavenums.shape[0], 1), 1.0 / math.sqrt(points), jnp.float32)
    return jnp.stack([factor * jnp.cos(angles), -factor * jnp.sin(angles)], axis=1).astype(
        jnp.bfloat16
    )


def forcing(grid_fields):
    flattened = grid_fields.reshape(FIELDS, -1)
    return (flattened * jnp.roll(flattened, -1, axis=0)).reshape(grid_fields.shape)


def coarse_columns(grid_fields):
    feat_width = grid_fields.shape[0]
    lat_rows = grid_fields.shape[1]
    lon_count = grid_fields.shape[2]
    blocks = grid_fields.reshape(feat_width, lat_rows // 2, 2, lon_count // 4, 4).mean(axis=(2, 4))
    return blocks.reshape(feat_width, -1).T.astype(jnp.bfloat16)


def spread_back(values, lat_rows):
    feat_width = values.shape[1]
    coarse = values.astype(jnp.float32).T.reshape(feat_width, lat_rows // 2, -1)
    before = jnp.roll(coarse, 1, axis=2)
    following = jnp.roll(coarse, -1, axis=2)
    pieces = [
        0.375 * before + 0.625 * coarse,
        0.125 * before + 0.875 * coarse,
        0.875 * coarse + 0.125 * following,
        0.625 * coarse + 0.375 * following,
    ]
    fine_grid = jnp.stack(pieces, axis=3).reshape(feat_width, lat_rows // 2, -1)
    return jnp.repeat(fine_grid, 2, axis=1)


def slot_positions(regimes, experts_total):
    onehot = (regimes[:, :, None] == jnp.arange(experts_total, dtype=jnp.int32)).astype(jnp.int32)
    ranking = jnp.cumsum(onehot, axis=1) - 1
    return jnp.sum(ranking * onehot, axis=2)


def network(columns, weight_in, weight_mid, weight_out):
    hidden = jax.nn.silu(jnp.dot(columns, weight_in, preferred_element_type=jnp.float32)).astype(
        jnp.bfloat16
    )
    deeper = jax.nn.silu(jnp.dot(hidden, weight_mid, preferred_element_type=jnp.float32)).astype(
        jnp.bfloat16
    )
    return jnp.dot(deeper, weight_out, preferred_element_type=jnp.float32).astype(jnp.bfloat16)


def masked_inverse(spectral, legendre, side_mask):
    masked = jnp.where(side_mask[:, :, :, None], spectral[:, None], jnp.zeros((), jnp.bfloat16))
    return jnp.einsum("psjc,pjl->pscl", masked, legendre, preferred_element_type=jnp.float32)


def masked_forward(legendre, coeffs, side_mask):
    both_sides = jnp.einsum(
        "pjl,pskrl->psjkr", legendre, coeffs, preferred_element_type=jnp.float32
    )
    return jnp.sum(jnp.where(side_mask[:, :, :, None, None], both_sides, 0.0), axis=1)


def on_device_arrays(spectral, legendre, pair_low, routes, w_in, w_mid, w_out):
    pair_count = spectral.shape[0]
    degrees = spectral.shape[1]
    channels = spectral.shape[2]
    feat_width = channels // 2
    lat_total = legendre.shape[2]
    wave_total = degrees - 1
    devices = lax.axis_size("wave")
    local_low = lax.dynamic_slice_in_dim(pair_low, lax.axis_index("wave") * pair_count, pair_count)
    side_mask = side_masks(local_low, wave_total)
    inverse_out = masked_inverse(spectral, legendre, side_mask)
    fourier_in = inverse_out.astype(jnp.bfloat16).reshape(2 * pair_count, feat_width, 2, lat_total)
    wavenums = slot_waves(pair_low, wave_total)
    inverse_table = fourier_table(wavenums, NLON, True)
    grid_fields = jnp.einsum(
        "qkra,qrl->kal",
        lax.all_to_all(fourier_in, "wave", split_axis=3, concat_axis=0, tiled=True),
        inverse_table,
        preferred_element_type=jnp.float32,
    )
    lat_rows = grid_fields.shape[1]
    forced = forcing(grid_fields)
    columns = coarse_columns(grid_fields)
    regimes = routes[:, 0].reshape(1, -1)
    positions = slot_positions(regimes, devices)[0]
    regime_row = regimes[0]
    capacity = 2 * columns.shape[0] // devices
    outgoing = (
        jnp.zeros((devices, capacity, feat_width), jnp.bfloat16)
        .at[regime_row, positions]
        .set(columns)
    )
    arrived = lax.all_to_all(outgoing, "wave", split_axis=0, concat_axis=0, tiled=True)
    answers = network(arrived.reshape(-1, feat_width), w_in[0], w_mid[0], w_out[0]).reshape(
        arrived.shape
    )
    incoming = lax.all_to_all(answers, "wave", split_axis=0, concat_axis=0, tiled=True)
    returned = incoming[regime_row, positions]
    correction = spread_back(returned, lat_rows)
    tendency_grid = (forced + correction).astype(jnp.bfloat16)
    forward_table = fourier_table(wavenums, NLON, False)
    fourier_out = jnp.einsum(
        "fal,qrl->qfra", tendency_grid, forward_table, preferred_element_type=jnp.float32
    ).astype(jnp.bfloat16)
    received = lax.all_to_all(fourier_out, "wave", split_axis=0, concat_axis=3, tiled=True)
    coeffs = received.reshape(pair_count, 2, received.shape[1], 2, received.shape[3])
    result = masked_forward(legendre, coeffs, side_mask)
    spectral_out = result.astype(jnp.bfloat16)
    return spectral_out.reshape(pair_count, degrees, channels)


def cost(flops, moved):
    return pl.CostEstimate(flops=int(flops), bytes_accessed=int(moved), transcendentals=0)


def channel_order(channels):
    source = jnp.arange(channels, dtype=jnp.int32)
    target = source % 2 * (channels // 2) + source // 2
    return (target[:, None] == source[None, :]).astype(jnp.bfloat16)


def inverse_kernel(spans, devices, low_ref, spectral_ref, legendre_ref, order_ref, *rest):
    outs, scratch = rest[:-1], rest[-1]
    step = pl.program_id(0)
    degrees, channels = spectral_ref.shape[1:]
    lat_total = legendre_ref.shape[2]
    rows = 2 * PAIR_STEP
    degree = lax.broadcasted_iota(jnp.int32, (degrees, channels), 0)
    for i in range(PAIR_STEP):
        low = low_ref[step * PAIR_STEP + i]
        ordered = jnp.dot(spectral_ref[i], order_ref[...], preferred_element_type=jnp.float32)
        lower = degree < degrees - 1 - low
        sides = jnp.concatenate(
            [jnp.where(lower, ordered, 0.0), jnp.where(lower, 0.0, ordered)], axis=1
        ).astype(jnp.bfloat16)
        result = lax.dot_general(
            legendre_ref[i], sides, (((0,), (0,)), ((), ())), preferred_element_type=jnp.float32
        )
        for s in range(2):
            for h in range(channels // 128):
                at = s * channels + h * 128
                scratch[h, pl.ds(2 * i + s, lat_total, stride=rows), :] = result[:, at : at + 128]
    per_device = lat_total // devices
    for out, (first, count) in zip(outs, spans):
        for d in range(devices):
            for h in range(channels // 128):
                block = scratch[h, pl.ds((d * per_device + first) * rows, count * rows), :]
                out[d, :, :, h * 128 : (h + 1) * 128] = block.reshape(count, rows, 128).astype(
                    jnp.bfloat16
                )


def inverse_legendre(spectral, legendre, local_low, order, spans, devices):
    pair_count, degrees, channels = spectral.shape
    lat_total = legendre.shape[2]
    rows = 2 * PAIR_STEP
    return pl.pallas_call(
        functools.partial(inverse_kernel, spans, devices),
        grid_spec=pltpu.PrefetchScalarGridSpec(
            num_scalar_prefetch=1,
            grid=(pair_count // PAIR_STEP,),
            in_specs=[
                pl.BlockSpec((PAIR_STEP, degrees, channels), lambda g, low: (g, 0, 0)),
                pl.BlockSpec((PAIR_STEP, degrees, lat_total), lambda g, low: (g, 0, 0)),
                pl.BlockSpec((channels, channels), lambda g, low: (0, 0)),
            ],
            out_specs=[
                pl.BlockSpec((devices, count, rows, channels), lambda g, low: (0, 0, g, 0))
                for _, count in spans
            ],
            scratch_shapes=[pltpu.VMEM((channels // 128, lat_total * rows, 128), jnp.float32)],
        ),
        out_shape=[
            jax.ShapeDtypeStruct((devices, count, 2 * pair_count, channels), jnp.bfloat16)
            for _, count in spans
        ],
        name="inverse_legendre",
        cost_estimate=cost(
            4 * pair_count * degrees * lat_total * channels, 2 * spectral.size * 2 + 2 * legendre.size
        ),
    )(local_low, spectral, legendre, order)


def grid_kernel(coeff_ref, table_ref, forced_ref, columns_ref, pooled):
    devices, lats, slots, channels = coeff_ref.shape
    feat = channels // 2
    rights = []
    for t in range(lats):
        waves = coeff_ref[:, t].astype(jnp.float32).reshape(devices * slots, channels)
        rights.append(
            jnp.concatenate([waves[:, :feat], waves[:, feat:]], axis=0).astype(jnp.bfloat16)
        )
    fields = jnp.dot(
        table_ref[...], jnp.concatenate(rights, axis=1), preferred_element_type=jnp.float32
    )
    total = None
    for t in range(lats):
        one = fields[:, t * feat : (t + 1) * feat]
        forced_ref[t] = one * pltpu.roll(one, feat - feat // 4, 1)
        total = one if total is None else total + one
    pooled[...] = total
    count = columns_ref.shape[0]
    spread = total.shape[0] // count
    mean = pooled[pl.ds(0, count, stride=spread), :]
    for u in range(1, spread):
        mean = mean + pooled[pl.ds(u, count, stride=spread), :]
    columns_ref[...] = (mean * (1.0 / (spread * lats))).astype(jnp.bfloat16)


def to_grid(coeffs, table):
    devices, lats, slots, channels = coeffs.shape
    points = table.shape[0]
    feat = channels // 2
    return pl.pallas_call(
        grid_kernel,
        grid=(lats // 2,),
        in_specs=[
            pl.BlockSpec((devices, 2, slots, channels), lambda i: (0, i, 0, 0)),
            pl.BlockSpec(table.shape, lambda i: (0, 0)),
        ],
        out_specs=[
            pl.BlockSpec((2, points, feat), lambda i: (i, 0, 0)),
            pl.BlockSpec((points // 4, feat), lambda i: (i, 0)),
        ],
        out_shape=[
            jax.ShapeDtypeStruct((lats, points, feat), jnp.float32),
            jax.ShapeDtypeStruct((lats // 2 * (points // 4), feat), jnp.bfloat16),
        ],
        scratch_shapes=[pltpu.VMEM((points, feat), jnp.float32)],
        name="to_grid",
        cost_estimate=cost(2 * coeffs.size * points, 2 * coeffs.size + 2 * table.size),
    )(coeffs, table)


def fourier_kernel(forced_ref, returned_ref, table_ref, out_ref, fine):
    lats, points, feat = forced_ref.shape
    devices, _, slots, _ = out_ref.shape
    coarse = returned_ref[...].astype(jnp.float32)
    count = coarse.shape[0]
    before = pltpu.roll(coarse, 1, 0)
    following = pltpu.roll(coarse, count - 1, 0)
    pieces = [
        0.375 * before + 0.625 * coarse,
        0.125 * before + 0.875 * coarse,
        0.875 * coarse + 0.125 * following,
        0.625 * coarse + 0.375 * following,
    ]
    for u, piece in enumerate(pieces):
        fine[pl.ds(u, count, stride=4), :] = piece
    correction = fine[...]
    right = jnp.concatenate(
        [(forced_ref[t] + correction).astype(jnp.bfloat16) for t in range(lats)], axis=1
    )
    waves = jnp.dot(table_ref[...], right, preferred_element_type=jnp.float32)
    half = devices * slots
    for t in range(lats):
        for r in range(2):
            part = waves[r * half : (r + 1) * half, t * feat : (t + 1) * feat]
            out_ref[:, t, :, r * feat : (r + 1) * feat] = part.reshape(devices, slots, feat).astype(
                jnp.bfloat16
            )


def to_fourier(forced, returned, table, devices):
    lats, points, feat = forced.shape
    slots = table.shape[0] // (2 * devices)
    return pl.pallas_call(
        fourier_kernel,
        grid=(lats // 2,),
        in_specs=[
            pl.BlockSpec((2, points, feat), lambda i: (i, 0, 0)),
            pl.BlockSpec((points // 4, feat), lambda i: (i, 0)),
            pl.BlockSpec(table.shape, lambda i: (0, 0)),
        ],
        out_specs=pl.BlockSpec((devices, 2, slots, 2 * feat), lambda i: (0, i, 0, 0)),
        out_shape=jax.ShapeDtypeStruct((devices, lats, slots, 2 * feat), jnp.bfloat16),
        scratch_shapes=[pltpu.VMEM((points, feat), jnp.float32)],
        name="to_fourier",
        cost_estimate=cost(2 * forced.size * table.shape[0], 4 * forced.size + 2 * table.size),
    )(forced, returned, table)


def forward_kernel(spans, low_ref, legendre_ref, order_ref, *rest):
    coeffs, out_ref, scratch = rest[:-2], rest[-2], rest[-1]
    step = pl.program_id(0)
    _, degrees, channels = out_ref.shape
    lat_total = legendre_ref.shape[2]
    rows = 2 * PAIR_STEP
    devices = coeffs[0].shape[0]
    per_device = lat_total // devices
    for ref, (first, count) in zip(coeffs, spans):
        for d in range(devices):
            block = ref[d].astype(jnp.float32).reshape(count * rows, channels)
            for h in range(channels // 128):
                scratch[h, pl.ds((d * per_device + first) * rows, count * rows), :] = block[
                    :, h * 128 : (h + 1) * 128
                ]
    degree = lax.broadcasted_iota(jnp.int32, (degrees, channels), 0)
    for i in range(PAIR_STEP):
        low = low_ref[step * PAIR_STEP + i]
        sides = []
        for s in range(2):
            side = jnp.concatenate(
                [
                    scratch[h, pl.ds(2 * i + s, lat_total, stride=rows), :]
                    for h in range(channels // 128)
                ],
                axis=1,
            ).astype(jnp.bfloat16)
            sides.append(
                lax.dot_general(
                    side,
                    order_ref[...],
                    (((1,), (1,)), ((), ())),
                    preferred_element_type=jnp.float32,
                ).astype(jnp.bfloat16)
            )
        both = jnp.dot(
            legendre_ref[i], jnp.concatenate(sides, axis=1), preferred_element_type=jnp.float32
        )
        lower = degree < degrees - 1 - low
        out_ref[i] = jnp.where(lower, both[:, :channels], both[:, channels:]).astype(jnp.bfloat16)


def forward_legendre(coeffs, legendre, local_low, order, spans):
    pair_count, degrees, lat_total = legendre.shape
    channels = order.shape[0]
    rows = 2 * PAIR_STEP
    devices = coeffs[0].shape[0]
    return pl.pallas_call(
        functools.partial(forward_kernel, spans),
        grid_spec=pltpu.PrefetchScalarGridSpec(
            num_scalar_prefetch=1,
            grid=(pair_count // PAIR_STEP,),
            in_specs=[
                pl.BlockSpec((PAIR_STEP, degrees, lat_total), lambda g, low: (g, 0, 0)),
                pl.BlockSpec((channels, channels), lambda g, low: (0, 0)),
            ]
            + [
                pl.BlockSpec((devices, count, rows, channels), lambda g, low: (0, 0, g, 0))
                for _, count in spans
            ],
            out_specs=pl.BlockSpec((PAIR_STEP, degrees, channels), lambda g, low: (g, 0, 0)),
            scratch_shapes=[pltpu.VMEM((channels // 128, lat_total * rows, 128), jnp.float32)],
        ),
        out_shape=jax.ShapeDtypeStruct((pair_count, degrees, channels), jnp.bfloat16),
        name="forward_legendre",
        cost_estimate=cost(
            4 * pair_count * degrees * lat_total * channels, 4 * legendre.size
        ),
    )(local_low, legendre, order, *coeffs)


def smooth(values):
    half = 0.5 * values
    return half + half * jnp.tanh(half)


def network_kernel(rows_ref, in_ref, mid_ref, out_w_ref, out_ref):
    sources, slots, feat = rows_ref.shape
    rows = rows_ref[...].reshape(sources * slots, feat)
    hidden = smooth(jnp.dot(rows, in_ref[0], preferred_element_type=jnp.float32))
    deeper = smooth(
        jnp.dot(hidden.astype(jnp.bfloat16), mid_ref[0], preferred_element_type=jnp.float32)
    )
    answer = jnp.dot(
        deeper.astype(jnp.bfloat16), out_w_ref[0], preferred_element_type=jnp.float32
    )
    out_ref[...] = answer.reshape(sources, slots, feat).astype(jnp.bfloat16)


def run_network(arrived, w_in, w_mid, w_out):
    devices, slots, feat = arrived.shape
    group = math.gcd(devices, 4)
    return pl.pallas_call(
        network_kernel,
        grid=(devices // group,),
        in_specs=[
            pl.BlockSpec((group, slots, feat), lambda i: (i, 0, 0)),
            pl.BlockSpec(w_in.shape, lambda i: (0, 0, 0)),
            pl.BlockSpec(w_mid.shape, lambda i: (0, 0, 0)),
            pl.BlockSpec(w_out.shape, lambda i: (0, 0, 0)),
        ],
        out_specs=pl.BlockSpec((group, slots, feat), lambda i: (i, 0, 0)),
        out_shape=jax.ShapeDtypeStruct(arrived.shape, jnp.bfloat16),
        name="network",
        cost_estimate=cost(
            2 * devices * slots * (w_in.size + w_mid.size + w_out.size), 4 * arrived.size + 2 * w_mid.size
        ),
    )(arrived, w_in, w_mid, w_out)


def phase_tables(wavenums, points):
    longitude = jnp.arange(points, dtype=jnp.int32)
    turn = jnp.float32(2.0 * math.pi / points)
    angles = (wavenums[:, None] * longitude[None, :] % points).astype(jnp.float32) * turn
    scale = jnp.float32(1.0 / math.sqrt(points))
    forward = jnp.concatenate([scale * jnp.cos(angles), -scale * jnp.sin(angles)], axis=0).astype(
        jnp.bfloat16
    )
    angles = (longitude[:, None] * wavenums[None, :] % points).astype(jnp.float32) * turn
    factor = jnp.where(wavenums == 0, jnp.float32(1.0), jnp.float32(2.0))[None, :]
    inverse = jnp.concatenate([factor * jnp.cos(angles), -factor * jnp.sin(angles)], axis=1).astype(
        jnp.bfloat16
    )
    return inverse, forward


def exchange(values):
    return lax.all_to_all(values, "wave", split_axis=0, concat_axis=0, tiled=True)


def row_spans(lat_rows):
    pairs = lat_rows // 2
    parts = math.gcd(pairs, ROW_PARTS)
    count = pairs // parts * 2
    return [(part * count, count) for part in range(parts)]


def on_device_kernels(spectral, legendre, pair_low, routes, w_in, w_mid, w_out):
    pair_count, degrees, channels = spectral.shape
    feat = channels // 2
    lat_total = legendre.shape[2]
    wave_total = degrees - 1
    devices = lax.axis_size("wave")
    lat_rows = lat_total // devices
    spans = row_spans(lat_rows)
    local_low = lax.dynamic_slice_in_dim(pair_low, lax.axis_index("wave") * pair_count, pair_count)
    order = channel_order(channels)
    sent = inverse_legendre(spectral, legendre, local_low, order, spans, devices)
    inverse_table, forward_table = phase_tables(slot_waves(pair_low, wave_total), NLON)
    regimes = routes[:, 0]
    total_columns = regimes.shape[0]
    positions = slot_positions(regimes.reshape(1, -1), devices)[0]
    capacity = 2 * total_columns // devices
    slots = capacity // SLOT_PARTS
    places = (positions // slots * devices + regimes) * slots + positions % slots
    outgoing = jnp.zeros((SLOT_PARTS * devices * slots, feat), jnp.bfloat16)
    forced = []
    width = NLON // 4
    for part, (first, count) in zip(sent, spans):
        forced_part, columns = to_grid(exchange(part), inverse_table)
        forced.append(forced_part)
        at = places[first // 2 * width : (first + count) // 2 * width]
        outgoing = outgoing.at[at].set(columns, unique_indices=True, mode="promise_in_bounds")
    outgoing = outgoing.reshape(SLOT_PARTS, devices, slots, feat)
    answers = [
        exchange(run_network(exchange(outgoing[part]), w_in, w_mid, w_out))
        for part in range(SLOT_PARTS)
    ]
    incoming = jnp.concatenate(answers, axis=0).reshape(-1, feat)
    received = []
    for forced_part, (first, count) in zip(forced, spans):
        at = places[first // 2 * width : (first + count) // 2 * width]
        returned = incoming.at[at].get(mode="promise_in_bounds")
        received.append(exchange(to_fourier(forced_part, returned, forward_table, devices)))
    return forward_legendre(received, legendre, local_low, order, spans)


def on_device(spectral, legendre, pair_low, routes, w_in, w_mid, w_out):
    devices = lax.axis_size("wave")
    aligned = (
        spectral.shape[0] % PAIR_STEP == 0
        and 2 * spectral.shape[0] % 8 == 0
        and legendre.shape[2] // devices % 2 == 0
        and 2 * routes.shape[0] // devices % (8 * SLOT_PARTS) == 0
    )
    body = on_device_kernels if aligned else on_device_arrays
    return body(spectral, legendre, pair_low, routes, w_in, w_mid, w_out)


def solution(mesh):
    placed = (
        P(("grp", "wave"), None, None),
        P("wave", None, None),
        P(),
        P(("grp", "wave"), None),
        P("wave", None, None),
        P("wave", None, None),
        P("wave", None, None),
    )
    return jax.shard_map(
        on_device,
        mesh=mesh,
        in_specs=placed,
        out_specs=P(("grp", "wave"), None, None),
        check_vma=False,
    )
```

```python
import functools
import math

import jax
import jax.numpy as jnp
from jax import lax
from jax.experimental import pallas as pl
from jax.experimental.pallas import tpu as pltpu
from jax.sharding import PartitionSpec as P

NLON = 1280
FIELDS = 4
PAIR_STEP = 4
SLOT_PARTS = 2


def slot_waves(pair_low, wave_total):
    return jnp.stack([pair_low, wave_total - 1 - pair_low], axis=1).reshape(-1)


def side_masks(pair_low, wave_total):
    degree = jnp.arange(wave_total + 1, dtype=jnp.int32)
    lower_side = degree[None, :] < (wave_total - pair_low)[:, None]
    return jnp.stack([lower_side, jnp.logical_not(lower_side)], axis=1)


def fourier_table(wavenums, points, inverse):
    longitude = jnp.arange(points, dtype=jnp.int32)
    phases = wavenums[:, None] * longitude[None, :] % points
    angles = phases.astype(jnp.float32) * jnp.float32(2.0 * math.pi / points)
    if inverse:
        factor = jnp.where(wavenums == 0, jnp.float32(1.0), jnp.float32(2.0))[:, None]
    else:
        factor = jnp.full((wavenums.shape[0], 1), 1.0 / math.sqrt(points), jnp.float32)
    return jnp.stack([factor * jnp.cos(angles), -factor * jnp.sin(angles)], axis=1).astype(
        jnp.bfloat16
    )


def forcing(grid_fields):
    flattened = grid_fields.reshape(FIELDS, -1)
    return (flattened * jnp.roll(flattened, -1, axis=0)).reshape(grid_fields.shape)


def coarse_columns(grid_fields):
    feat_width = grid_fields.shape[0]
    lat_rows = grid_fields.shape[1]
    lon_count = grid_fields.shape[2]
    blocks = grid_fields.reshape(feat_width, lat_rows // 2, 2, lon_count // 4, 4).mean(axis=(2, 4))
    return blocks.reshape(feat_width, -1).T.astype(jnp.bfloat16)


def spread_back(values, lat_rows):
    feat_width = values.shape[1]
    coarse = values.astype(jnp.float32).T.reshape(feat_width, lat_rows // 2, -1)
    before = jnp.roll(coarse, 1, axis=2)
    following = jnp.roll(coarse, -1, axis=2)
    pieces = [
        0.375 * before + 0.625 * coarse,
        0.125 * before + 0.875 * coarse,
        0.875 * coarse + 0.125 * following,
        0.625 * coarse + 0.375 * following,
    ]
    fine_grid = jnp.stack(pieces, axis=3).reshape(feat_width, lat_rows // 2, -1)
    return jnp.repeat(fine_grid, 2, axis=1)


def slot_positions(regimes, experts_total):
    onehot = (regimes[:, :, None] == jnp.arange(experts_total, dtype=jnp.int32)).astype(jnp.int32)
    ranking = jnp.cumsum(onehot, axis=1) - 1
    return jnp.sum(ranking * onehot, axis=2)


def network(columns, weight_in, weight_mid, weight_out):
    hidden = jax.nn.silu(jnp.dot(columns, weight_in, preferred_element_type=jnp.float32)).astype(
        jnp.bfloat16
    )
    deeper = jax.nn.silu(jnp.dot(hidden, weight_mid, preferred_element_type=jnp.float32)).astype(
        jnp.bfloat16
    )
    return jnp.dot(deeper, weight_out, preferred_element_type=jnp.float32).astype(jnp.bfloat16)


def masked_inverse(spectral, legendre, side_mask):
    masked = jnp.where(side_mask[:, :, :, None], spectral[:, None], jnp.zeros((), jnp.bfloat16))
    return jnp.einsum("psjc,pjl->pscl", masked, legendre, preferred_element_type=jnp.float32)


def masked_forward(legendre, coeffs, side_mask):
    both_sides = jnp.einsum(
        "pjl,pskrl->psjkr", legendre, coeffs, preferred_element_type=jnp.float32
    )
    return jnp.sum(jnp.where(side_mask[:, :, :, None, None], both_sides, 0.0), axis=1)


def on_device_arrays(spectral, legendre, pair_low, routes, w_in, w_mid, w_out):
    pair_count = spectral.shape[0]
    degrees = spectral.shape[1]
    channels = spectral.shape[2]
    feat_width = channels // 2
    lat_total = legendre.shape[2]
    wave_total = degrees - 1
    devices = lax.axis_size("wave")
    local_low = lax.dynamic_slice_in_dim(pair_low, lax.axis_index("wave") * pair_count, pair_count)
    side_mask = side_masks(local_low, wave_total)
    inverse_out = masked_inverse(spectral, legendre, side_mask)
    fourier_in = inverse_out.astype(jnp.bfloat16).reshape(2 * pair_count, feat_width, 2, lat_total)
    wavenums = slot_waves(pair_low, wave_total)
    inverse_table = fourier_table(wavenums, NLON, True)
    grid_fields = jnp.einsum(
        "qkra,qrl->kal",
        lax.all_to_all(fourier_in, "wave", split_axis=3, concat_axis=0, tiled=True),
        inverse_table,
        preferred_element_type=jnp.float32,
    )
    lat_rows = grid_fields.shape[1]
    forced = forcing(grid_fields)
    columns = coarse_columns(grid_fields)
    regimes = routes[:, 0].reshape(1, -1)
    positions = slot_positions(regimes, devices)[0]
    regime_row = regimes[0]
    capacity = 2 * columns.shape[0] // devices
    outgoing = (
        jnp.zeros((devices, capacity, feat_width), jnp.bfloat16)
        .at[regime_row, positions]
        .set(columns)
    )
    arrived = lax.all_to_all(outgoing, "wave", split_axis=0, concat_axis=0, tiled=True)
    answers = network(arrived.reshape(-1, feat_width), w_in[0], w_mid[0], w_out[0]).reshape(
        arrived.shape
    )
    incoming = lax.all_to_all(answers, "wave", split_axis=0, concat_axis=0, tiled=True)
    returned = incoming[regime_row, positions]
    correction = spread_back(returned, lat_rows)
    tendency_grid = (forced + correction).astype(jnp.bfloat16)
    forward_table = fourier_table(wavenums, NLON, False)
    fourier_out = jnp.einsum(
        "fal,qrl->qfra", tendency_grid, forward_table, preferred_element_type=jnp.float32
    ).astype(jnp.bfloat16)
    received = lax.all_to_all(fourier_out, "wave", split_axis=0, concat_axis=3, tiled=True)
    coeffs = received.reshape(pair_count, 2, received.shape[1], 2, received.shape[3])
    result = masked_forward(legendre, coeffs, side_mask)
    spectral_out = result.astype(jnp.bfloat16)
    return spectral_out.reshape(pair_count, degrees, channels)


def cost(flops, moved):
    return pl.CostEstimate(flops=int(flops), bytes_accessed=int(moved), transcendentals=0)


def channel_order(channels):
    source = jnp.arange(channels, dtype=jnp.int32)
    target = source % 2 * (channels // 2) + source // 2
    return (target[:, None] == source[None, :]).astype(jnp.bfloat16)


def inverse_kernel(spans, devices, low_ref, spectral_ref, legendre_ref, order_ref, *rest):
    outs, scratch = rest[:-1], rest[-1]
    step = pl.program_id(0)
    degrees, channels = spectral_ref.shape[1:]
    lat_total = legendre_ref.shape[1]
    rows = 2 * PAIR_STEP
    degree = lax.broadcasted_iota(jnp.int32, (degrees, channels), 0)
    for i in range(PAIR_STEP):
        low = low_ref[step * PAIR_STEP + i]
        ordered = jnp.dot(spectral_ref[i], order_ref[...], preferred_element_type=jnp.float32)
        lower = degree < degrees - 1 - low
        sides = jnp.concatenate(
            [jnp.where(lower, ordered, 0.0), jnp.where(lower, 0.0, ordered)], axis=1
        ).astype(jnp.bfloat16)
        result = jnp.dot(legendre_ref[i], sides, preferred_element_type=jnp.float32)
        for s in range(2):
            for h in range(channels // 128):
                at = s * channels + h * 128
                scratch[h, pl.ds(2 * i + s, lat_total, stride=rows), :] = result[:, at : at + 128]
    per_device = lat_total // devices
    for out, (first, count) in zip(outs, spans):
        for d in range(devices):
            for h in range(channels // 128):
                block = scratch[h, pl.ds((d * per_device + first) * rows, count * rows), :]
                out[d, :, :, h * 128 : (h + 1) * 128] = block.reshape(count, rows, 128).astype(
                    jnp.bfloat16
                )


def inverse_legendre(spectral, legendre, local_low, order, spans, devices):
    pair_count, degrees, channels = spectral.shape
    lat_total = legendre.shape[1]
    rows = 2 * PAIR_STEP
    return pl.pallas_call(
        functools.partial(inverse_kernel, spans, devices),
        grid_spec=pltpu.PrefetchScalarGridSpec(
            num_scalar_prefetch=1,
            grid=(pair_count // PAIR_STEP,),
            in_specs=[
                pl.BlockSpec((PAIR_STEP, degrees, channels), lambda g, low: (g, 0, 0)),
                pl.BlockSpec((PAIR_STEP, lat_total, degrees), lambda g, low: (g, 0, 0)),
                pl.BlockSpec((channels, channels), lambda g, low: (0, 0)),
            ],
            out_specs=[
                pl.BlockSpec((devices, count, rows, channels), lambda g, low: (0, 0, g, 0))
                for _, count in spans
            ],
            scratch_shapes=[pltpu.VMEM((channels // 128, lat_total * rows, 128), jnp.float32)],
        ),
        out_shape=[
            jax.ShapeDtypeStruct((devices, count, 2 * pair_count, channels), jnp.bfloat16)
            for _, count in spans
        ],
        name="inverse_legendre",
        cost_estimate=cost(
            4 * pair_count * degrees * lat_total * channels, 2 * spectral.size * 2 + 2 * legendre.size
        ),
    )(local_low, spectral, legendre, order)


def grid_kernel(coeff_ref, table_ref, forced_ref, columns_ref, pooled):
    devices, lats, slots, channels = coeff_ref.shape
    feat = channels // 2
    rights = []
    for t in range(lats):
        waves = coeff_ref[:, t].astype(jnp.float32).reshape(devices * slots, channels)
        rights.append(
            jnp.concatenate([waves[:, :feat], waves[:, feat:]], axis=0).astype(jnp.bfloat16)
        )
    fields = jnp.dot(
        table_ref[...], jnp.concatenate(rights, axis=1), preferred_element_type=jnp.float32
    )
    total = None
    for t in range(lats):
        one = fields[:, t * feat : (t + 1) * feat]
        forced_ref[t] = one * pltpu.roll(one, feat - feat // 4, 1)
        total = one if total is None else total + one
    pooled[...] = total
    count = columns_ref.shape[0]
    spread = total.shape[0] // count
    mean = pooled[pl.ds(0, count, stride=spread), :]
    for u in range(1, spread):
        mean = mean + pooled[pl.ds(u, count, stride=spread), :]
    columns_ref[...] = (mean * (1.0 / (spread * lats))).astype(jnp.bfloat16)


def to_grid(coeffs, table):
    devices, lats, slots, channels = coeffs.shape
    points = table.shape[0]
    feat = channels // 2
    return pl.pallas_call(
        grid_kernel,
        grid=(lats // 2,),
        in_specs=[
            pl.BlockSpec((devices, 2, slots, channels), lambda i: (0, i, 0, 0)),
            pl.BlockSpec(table.shape, lambda i: (0, 0)),
        ],
        out_specs=[
            pl.BlockSpec((2, points, feat), lambda i: (i, 0, 0)),
            pl.BlockSpec((points // 4, feat), lambda i: (i, 0)),
        ],
        out_shape=[
            jax.ShapeDtypeStruct((lats, points, feat), jnp.float32),
            jax.ShapeDtypeStruct((lats // 2 * (points // 4), feat), jnp.bfloat16),
        ],
        scratch_shapes=[pltpu.VMEM((points, feat), jnp.float32)],
        name="to_grid",
        cost_estimate=cost(2 * coeffs.size * points, 2 * coeffs.size + 2 * table.size),
    )(coeffs, table)


def fourier_kernel(forced_ref, returned_ref, table_ref, out_ref, fine):
    lats, points, feat = forced_ref.shape
    devices, _, slots, _ = out_ref.shape
    coarse = returned_ref[...].astype(jnp.float32)
    count = coarse.shape[0]
    before = pltpu.roll(coarse, 1, 0)
    following = pltpu.roll(coarse, count - 1, 0)
    pieces = [
        0.375 * before + 0.625 * coarse,
        0.125 * before + 0.875 * coarse,
        0.875 * coarse + 0.125 * following,
        0.625 * coarse + 0.375 * following,
    ]
    for u, piece in enumerate(pieces):
        fine[pl.ds(u, count, stride=4), :] = piece
    correction = fine[...]
    right = jnp.concatenate(
        [(forced_ref[t] + correction).astype(jnp.bfloat16) for t in range(lats)], axis=1
    )
    waves = jnp.dot(table_ref[...], right, preferred_element_type=jnp.float32)
    half = devices * slots
    for t in range(lats):
        for r in range(2):
            part = waves[r * half : (r + 1) * half, t * feat : (t + 1) * feat]
            out_ref[:, t, :, r * feat : (r + 1) * feat] = part.reshape(devices, slots, feat).astype(
                jnp.bfloat16
            )


def to_fourier(forced, returned, table, devices):
    lats, points, feat = forced.shape
    slots = table.shape[0] // (2 * devices)
    return pl.pallas_call(
        fourier_kernel,
        grid=(lats // 2,),
        in_specs=[
            pl.BlockSpec((2, points, feat), lambda i: (i, 0, 0)),
            pl.BlockSpec((points // 4, feat), lambda i: (i, 0)),
            pl.BlockSpec(table.shape, lambda i: (0, 0)),
        ],
        out_specs=pl.BlockSpec((devices, 2, slots, 2 * feat), lambda i: (0, i, 0, 0)),
        out_shape=jax.ShapeDtypeStruct((devices, lats, slots, 2 * feat), jnp.bfloat16),
        scratch_shapes=[pltpu.VMEM((points, feat), jnp.float32)],
        name="to_fourier",
        cost_estimate=cost(2 * forced.size * table.shape[0], 4 * forced.size + 2 * table.size),
    )(forced, returned, table)


def forward_kernel(spans, low_ref, legendre_ref, order_ref, *rest):
    coeffs, out_ref, scratch = rest[:-2], rest[-2], rest[-1]
    step = pl.program_id(0)
    _, degrees, channels = out_ref.shape
    lat_total = legendre_ref.shape[1]
    rows = 2 * PAIR_STEP
    devices = coeffs[0].shape[0]
    per_device = lat_total // devices
    for ref, (first, count) in zip(coeffs, spans):
        for d in range(devices):
            block = ref[d].astype(jnp.float32).reshape(count * rows, channels)
            for h in range(channels // 128):
                scratch[h, pl.ds((d * per_device + first) * rows, count * rows), :] = block[
                    :, h * 128 : (h + 1) * 128
                ]
    degree = lax.broadcasted_iota(jnp.int32, (degrees, channels), 0)
    for i in range(PAIR_STEP):
        low = low_ref[step * PAIR_STEP + i]
        sides = []
        for s in range(2):
            side = jnp.concatenate(
                [
                    scratch[h, pl.ds(2 * i + s, lat_total, stride=rows), :]
                    for h in range(channels // 128)
                ],
                axis=1,
            ).astype(jnp.bfloat16)
            sides.append(
                lax.dot_general(
                    side,
                    order_ref[...],
                    (((1,), (1,)), ((), ())),
                    preferred_element_type=jnp.float32,
                ).astype(jnp.bfloat16)
            )
        both = lax.dot_general(
            legendre_ref[i],
            jnp.concatenate(sides, axis=1),
            (((0,), (0,)), ((), ())),
            preferred_element_type=jnp.float32,
        )
        lower = degree < degrees - 1 - low
        out_ref[i] = jnp.where(lower, both[:, :channels], both[:, channels:]).astype(jnp.bfloat16)


def forward_legendre(coeffs, legendre, local_low, order, spans):
    pair_count, lat_total, degrees = legendre.shape
    channels = order.shape[0]
    rows = 2 * PAIR_STEP
    devices = coeffs[0].shape[0]
    return pl.pallas_call(
        functools.partial(forward_kernel, spans),
        grid_spec=pltpu.PrefetchScalarGridSpec(
            num_scalar_prefetch=1,
            grid=(pair_count // PAIR_STEP,),
            in_specs=[
                pl.BlockSpec((PAIR_STEP, lat_total, degrees), lambda g, low: (g, 0, 0)),
                pl.BlockSpec((channels, channels), lambda g, low: (0, 0)),
            ]
            + [
                pl.BlockSpec((devices, count, rows, channels), lambda g, low: (0, 0, g, 0))
                for _, count in spans
            ],
            out_specs=pl.BlockSpec((PAIR_STEP, degrees, channels), lambda g, low: (g, 0, 0)),
            scratch_shapes=[pltpu.VMEM((channels // 128, lat_total * rows, 128), jnp.float32)],
        ),
        out_shape=jax.ShapeDtypeStruct((pair_count, degrees, channels), jnp.bfloat16),
        name="forward_legendre",
        cost_estimate=cost(
            4 * pair_count * degrees * lat_total * channels, 4 * legendre.size
        ),
    )(local_low, legendre, order, *coeffs)


def smooth(values):
    half = 0.5 * values
    return half + half * jnp.tanh(half)


def network_kernel(rows_ref, in_ref, mid_ref, out_w_ref, out_ref):
    sources, slots, feat = rows_ref.shape
    rows = rows_ref[...].reshape(sources * slots, feat)
    hidden = smooth(jnp.dot(rows, in_ref[0], preferred_element_type=jnp.float32))
    deeper = smooth(
        jnp.dot(hidden.astype(jnp.bfloat16), mid_ref[0], preferred_element_type=jnp.float32)
    )
    answer = jnp.dot(
        deeper.astype(jnp.bfloat16), out_w_ref[0], preferred_element_type=jnp.float32
    )
    out_ref[...] = answer.reshape(sources, slots, feat).astype(jnp.bfloat16)


def run_network(arrived, w_in, w_mid, w_out):
    devices, slots, feat = arrived.shape
    group = math.gcd(devices, 4)
    return pl.pallas_call(
        network_kernel,
        grid=(devices // group,),
        in_specs=[
            pl.BlockSpec((group, slots, feat), lambda i: (i, 0, 0)),
            pl.BlockSpec(w_in.shape, lambda i: (0, 0, 0)),
            pl.BlockSpec(w_mid.shape, lambda i: (0, 0, 0)),
            pl.BlockSpec(w_out.shape, lambda i: (0, 0, 0)),
        ],
        out_specs=pl.BlockSpec((group, slots, feat), lambda i: (i, 0, 0)),
        out_shape=jax.ShapeDtypeStruct(arrived.shape, jnp.bfloat16),
        name="network",
        cost_estimate=cost(
            2 * devices * slots * (w_in.size + w_mid.size + w_out.size), 4 * arrived.size + 2 * w_mid.size
        ),
    )(arrived, w_in, w_mid, w_out)


def phase_tables(wavenums, points):
    longitude = jnp.arange(points, dtype=jnp.int32)
    turn = jnp.float32(2.0 * math.pi / points)
    angles = (wavenums[:, None] * longitude[None, :] % points).astype(jnp.float32) * turn
    scale = jnp.float32(1.0 / math.sqrt(points))
    forward = jnp.concatenate([scale * jnp.cos(angles), -scale * jnp.sin(angles)], axis=0).astype(
        jnp.bfloat16
    )
    angles = (longitude[:, None] * wavenums[None, :] % points).astype(jnp.float32) * turn
    factor = jnp.where(wavenums == 0, jnp.float32(1.0), jnp.float32(2.0))[None, :]
    inverse = jnp.concatenate([factor * jnp.cos(angles), -factor * jnp.sin(angles)], axis=1).astype(
        jnp.bfloat16
    )
    return inverse, forward


def exchange(values):
    return lax.all_to_all(values, "wave", split_axis=0, concat_axis=0, tiled=True)


def row_spans(lat_rows):
    pairs = lat_rows // 2
    first = max(1, pairs * 7 // 10)
    spans = [(0, 2 * first), (2 * first, 2 * (pairs - first))]
    return [span for span in spans if span[1] > 0]


def on_device_kernels(spectral, legendre, pair_low, routes, w_in, w_mid, w_out):
    pair_count, degrees, channels = spectral.shape
    feat = channels // 2
    lat_total = legendre.shape[2]
    wave_total = degrees - 1
    devices = lax.axis_size("wave")
    lat_rows = lat_total // devices
    spans = row_spans(lat_rows)
    local_low = lax.dynamic_slice_in_dim(pair_low, lax.axis_index("wave") * pair_count, pair_count)
    order = channel_order(channels)
    turned = jnp.swapaxes(legendre, 1, 2)
    sent = inverse_legendre(spectral, turned, local_low, order, spans, devices)
    pair_low, routes, *sent = lax.optimization_barrier((pair_low, routes, *sent))
    arriving = exchange(sent[0])
    inverse_table, forward_table = phase_tables(slot_waves(pair_low, wave_total), NLON)
    regimes = routes[:, 0]
    total_columns = regimes.shape[0]
    positions = slot_positions(regimes.reshape(1, -1), devices)[0]
    capacity = 2 * total_columns // devices
    slots = capacity // SLOT_PARTS
    places = (positions // slots * devices + regimes) * slots + positions % slots
    outgoing = jnp.zeros((SLOT_PARTS * devices * slots, feat), jnp.bfloat16)
    forced = []
    width = NLON // 4
    for part, (first, count) in enumerate(spans):
        held = (arriving, sent[part + 1 :], inverse_table, forward_table, places, outgoing)
        arriving, later, inverse_table, forward_table, places, outgoing = lax.optimization_barrier(
            held
        )
        arrived = arriving
        if later:
            sent[part + 1 :] = later
            arriving = exchange(sent[part + 1])
        forced_part, columns = to_grid(arrived, inverse_table)
        forced.append(forced_part)
        at = places[first // 2 * width : (first + count) // 2 * width]
        outgoing = outgoing.at[at].set(columns, unique_indices=True, mode="promise_in_bounds")
    outgoing = outgoing.reshape(SLOT_PARTS, devices, slots, feat)
    answers = [
        exchange(run_network(exchange(outgoing[part]), w_in, w_mid, w_out))
        for part in range(SLOT_PARTS)
    ]
    incoming = jnp.concatenate(answers, axis=0).reshape(-1, feat)
    received = [None] * len(spans)
    for part in reversed(range(len(spans))):
        first, count = spans[part]
        at = places[first // 2 * width : (first + count) // 2 * width]
        returned = incoming.at[at].get(mode="promise_in_bounds")
        received[part] = exchange(to_fourier(forced[part], returned, forward_table, devices))
    return forward_legendre(received, turned, local_low, order, spans)


def on_device(spectral, legendre, pair_low, routes, w_in, w_mid, w_out):
    devices = lax.axis_size("wave")
    aligned = (
        spectral.shape[0] % PAIR_STEP == 0
        and 2 * spectral.shape[0] % 8 == 0
        and legendre.shape[2] // devices % 2 == 0
        and 2 * routes.shape[0] // devices % (8 * SLOT_PARTS) == 0
    )
    body = on_device_kernels if aligned else on_device_arrays
    return body(spectral, legendre, pair_low, routes, w_in, w_mid, w_out)


def solution(mesh):
    placed = (
        P(("grp", "wave"), None, None),
        P("wave", None, None),
        P(),
        P(("grp", "wave"), None),
        P("wave", None, None),
        P("wave", None, None),
        P("wave", None, None),
    )
    return jax.shard_map(
        on_device,
        mesh=mesh,
        in_specs=placed,
        out_specs=P(("grp", "wave"), None, None),
        check_vma=False,
    )
```

```python
import functools
import math

import jax
import jax.numpy as jnp
from jax import lax
from jax.experimental import pallas as pl
from jax.experimental.pallas import tpu as pltpu
from jax.sharding import PartitionSpec as P

NLON = 1280
FIELDS = 4
PAIR_STEP = 4


def slot_waves(pair_low, wave_total):
    return jnp.stack([pair_low, wave_total - 1 - pair_low], axis=1).reshape(-1)


def side_masks(pair_low, wave_total):
    degree = jnp.arange(wave_total + 1, dtype=jnp.int32)
    lower_side = degree[None, :] < (wave_total - pair_low)[:, None]
    return jnp.stack([lower_side, jnp.logical_not(lower_side)], axis=1)


def fourier_table(wavenums, points, inverse):
    longitude = jnp.arange(points, dtype=jnp.int32)
    phases = wavenums[:, None] * longitude[None, :] % points
    angles = phases.astype(jnp.float32) * jnp.float32(2.0 * math.pi / points)
    if inverse:
        factor = jnp.where(wavenums == 0, jnp.float32(1.0), jnp.float32(2.0))[:, None]
    else:
        factor = jnp.full((wavenums.shape[0], 1), 1.0 / math.sqrt(points), jnp.float32)
    return jnp.stack([factor * jnp.cos(angles), -factor * jnp.sin(angles)], axis=1).astype(
        jnp.bfloat16
    )


def forcing(grid_fields):
    flattened = grid_fields.reshape(FIELDS, -1)
    return (flattened * jnp.roll(flattened, -1, axis=0)).reshape(grid_fields.shape)


def coarse_columns(grid_fields):
    feat_width = grid_fields.shape[0]
    lat_rows = grid_fields.shape[1]
    lon_count = grid_fields.shape[2]
    blocks = grid_fields.reshape(feat_width, lat_rows // 2, 2, lon_count // 4, 4).mean(axis=(2, 4))
    return blocks.reshape(feat_width, -1).T.astype(jnp.bfloat16)


def spread_back(values, lat_rows):
    feat_width = values.shape[1]
    coarse = values.astype(jnp.float32).T.reshape(feat_width, lat_rows // 2, -1)
    before = jnp.roll(coarse, 1, axis=2)
    following = jnp.roll(coarse, -1, axis=2)
    pieces = [
        0.375 * before + 0.625 * coarse,
        0.125 * before + 0.875 * coarse,
        0.875 * coarse + 0.125 * following,
        0.625 * coarse + 0.375 * following,
    ]
    fine_grid = jnp.stack(pieces, axis=3).reshape(feat_width, lat_rows // 2, -1)
    return jnp.repeat(fine_grid, 2, axis=1)


def slot_positions(regimes, experts_total):
    onehot = (regimes[:, :, None] == jnp.arange(experts_total, dtype=jnp.int32)).astype(jnp.int32)
    ranking = jnp.cumsum(onehot, axis=1) - 1
    return jnp.sum(ranking * onehot, axis=2)


def network(columns, weight_in, weight_mid, weight_out):
    hidden = jax.nn.silu(jnp.dot(columns, weight_in, preferred_element_type=jnp.float32)).astype(
        jnp.bfloat16
    )
    deeper = jax.nn.silu(jnp.dot(hidden, weight_mid, preferred_element_type=jnp.float32)).astype(
        jnp.bfloat16
    )
    return jnp.dot(deeper, weight_out, preferred_element_type=jnp.float32).astype(jnp.bfloat16)


def masked_inverse(spectral, legendre, side_mask):
    masked = jnp.where(side_mask[:, :, :, None], spectral[:, None], jnp.zeros((), jnp.bfloat16))
    return jnp.einsum("psjc,pjl->pscl", masked, legendre, preferred_element_type=jnp.float32)


def masked_forward(legendre, coeffs, side_mask):
    both_sides = jnp.einsum(
        "pjl,pskrl->psjkr", legendre, coeffs, preferred_element_type=jnp.float32
    )
    return jnp.sum(jnp.where(side_mask[:, :, :, None, None], both_sides, 0.0), axis=1)


def on_device_arrays(spectral, legendre, pair_low, routes, w_in, w_mid, w_out):
    pair_count = spectral.shape[0]
    degrees = spectral.shape[1]
    channels = spectral.shape[2]
    feat_width = channels // 2
    lat_total = legendre.shape[2]
    wave_total = degrees - 1
    devices = lax.axis_size("wave")
    local_low = lax.dynamic_slice_in_dim(pair_low, lax.axis_index("wave") * pair_count, pair_count)
    side_mask = side_masks(local_low, wave_total)
    inverse_out = masked_inverse(spectral, legendre, side_mask)
    fourier_in = inverse_out.astype(jnp.bfloat16).reshape(2 * pair_count, feat_width, 2, lat_total)
    wavenums = slot_waves(pair_low, wave_total)
    inverse_table = fourier_table(wavenums, NLON, True)
    grid_fields = jnp.einsum(
        "qkra,qrl->kal",
        lax.all_to_all(fourier_in, "wave", split_axis=3, concat_axis=0, tiled=True),
        inverse_table,
        preferred_element_type=jnp.float32,
    )
    lat_rows = grid_fields.shape[1]
    forced = forcing(grid_fields)
    columns = coarse_columns(grid_fields)
    regimes = routes[:, 0].reshape(1, -1)
    positions = slot_positions(regimes, devices)[0]
    regime_row = regimes[0]
    capacity = 2 * columns.shape[0] // devices
    outgoing = (
        jnp.zeros((devices, capacity, feat_width), jnp.bfloat16)
        .at[regime_row, positions]
        .set(columns)
    )
    arrived = lax.all_to_all(outgoing, "wave", split_axis=0, concat_axis=0, tiled=True)
    answers = network(arrived.reshape(-1, feat_width), w_in[0], w_mid[0], w_out[0]).reshape(
        arrived.shape
    )
    incoming = lax.all_to_all(answers, "wave", split_axis=0, concat_axis=0, tiled=True)
    returned = incoming[regime_row, positions]
    correction = spread_back(returned, lat_rows)
    tendency_grid = (forced + correction).astype(jnp.bfloat16)
    forward_table = fourier_table(wavenums, NLON, False)
    fourier_out = jnp.einsum(
        "fal,qrl->qfra", tendency_grid, forward_table, preferred_element_type=jnp.float32
    ).astype(jnp.bfloat16)
    received = lax.all_to_all(fourier_out, "wave", split_axis=0, concat_axis=3, tiled=True)
    coeffs = received.reshape(pair_count, 2, received.shape[1], 2, received.shape[3])
    result = masked_forward(legendre, coeffs, side_mask)
    spectral_out = result.astype(jnp.bfloat16)
    return spectral_out.reshape(pair_count, degrees, channels)


def cost(flops, moved):
    return pl.CostEstimate(flops=int(flops), bytes_accessed=int(moved), transcendentals=0)


def channel_order(channels):
    source = jnp.arange(channels, dtype=jnp.int32)
    target = source % 2 * (channels // 2) + source // 2
    return (target[:, None] == source[None, :]).astype(jnp.bfloat16)


def inverse_kernel(spans, devices, low_ref, spectral_ref, legendre_ref, order_ref, *rest):
    outs, scratch = rest[:-1], rest[-1]
    step = pl.program_id(0)
    degrees, channels = spectral_ref.shape[1:]
    lat_total = legendre_ref.shape[1]
    rows = 2 * PAIR_STEP
    degree = lax.broadcasted_iota(jnp.int32, (degrees, channels), 0)
    for i in range(PAIR_STEP):
        low = low_ref[step * PAIR_STEP + i]
        ordered = jnp.dot(spectral_ref[i], order_ref[...], preferred_element_type=jnp.float32)
        lower = degree < degrees - 1 - low
        sides = jnp.concatenate(
            [jnp.where(lower, ordered, 0.0), jnp.where(lower, 0.0, ordered)], axis=1
        ).astype(jnp.bfloat16)
        result = jnp.dot(legendre_ref[i], sides, preferred_element_type=jnp.float32)
        for s in range(2):
            for h in range(channels // 128):
                at = s * channels + h * 128
                scratch[h, pl.ds(2 * i + s, lat_total, stride=rows), :] = result[:, at : at + 128]
    per_device = lat_total // devices
    for out, (first, count) in zip(outs, spans):
        for d in range(devices):
            for h in range(channels // 128):
                block = scratch[h, pl.ds((d * per_device + first) * rows, count * rows), :]
                out[d, :, :, h * 128 : (h + 1) * 128] = block.reshape(count, rows, 128).astype(
                    jnp.bfloat16
                )


def inverse_legendre(spectral, legendre, local_low, order, spans, devices):
    pair_count, degrees, channels = spectral.shape
    lat_total = legendre.shape[1]
    rows = 2 * PAIR_STEP
    return pl.pallas_call(
        functools.partial(inverse_kernel, spans, devices),
        grid_spec=pltpu.PrefetchScalarGridSpec(
            num_scalar_prefetch=1,
            grid=(pair_count // PAIR_STEP,),
            in_specs=[
                pl.BlockSpec((PAIR_STEP, degrees, channels), lambda g, low: (g, 0, 0)),
                pl.BlockSpec((PAIR_STEP, lat_total, degrees), lambda g, low: (g, 0, 0)),
                pl.BlockSpec((channels, channels), lambda g, low: (0, 0)),
            ],
            out_specs=[
                pl.BlockSpec((devices, count, rows, channels), lambda g, low: (0, 0, g, 0))
                for _, count in spans
            ],
            scratch_shapes=[pltpu.VMEM((channels // 128, lat_total * rows, 128), jnp.float32)],
        ),
        out_shape=[
            jax.ShapeDtypeStruct((devices, count, 2 * pair_count, channels), jnp.bfloat16)
            for _, count in spans
        ],
        name="inverse_legendre",
        cost_estimate=cost(
            4 * pair_count * degrees * lat_total * channels, 2 * spectral.size * 2 + 2 * legendre.size
        ),
    )(local_low, spectral, legendre, order)


def grid_kernel(coeff_ref, table_ref, forced_ref, columns_ref, pooled):
    devices, lats, slots, channels = coeff_ref.shape
    feat = channels // 2
    rights = []
    for t in range(lats):
        waves = coeff_ref[:, t].astype(jnp.float32).reshape(devices * slots, channels)
        rights.append(
            jnp.concatenate([waves[:, :feat], waves[:, feat:]], axis=0).astype(jnp.bfloat16)
        )
    fields = jnp.dot(
        table_ref[...], jnp.concatenate(rights, axis=1), preferred_element_type=jnp.float32
    )
    total = None
    for t in range(lats):
        one = fields[:, t * feat : (t + 1) * feat]
        forced_ref[t] = one * pltpu.roll(one, feat - feat // 4, 1)
        total = one if total is None else total + one
    pooled[...] = total
    count = columns_ref.shape[0]
    spread = total.shape[0] // count
    mean = pooled[pl.ds(0, count, stride=spread), :]
    for u in range(1, spread):
        mean = mean + pooled[pl.ds(u, count, stride=spread), :]
    columns_ref[...] = (mean * (1.0 / (spread * lats))).astype(jnp.bfloat16)


def to_grid(coeffs, table):
    devices, lats, slots, channels = coeffs.shape
    points = table.shape[0]
    feat = channels // 2
    return pl.pallas_call(
        grid_kernel,
        grid=(lats // 2,),
        in_specs=[
            pl.BlockSpec((devices, 2, slots, channels), lambda i: (0, i, 0, 0)),
            pl.BlockSpec(table.shape, lambda i: (0, 0)),
        ],
        out_specs=[
            pl.BlockSpec((2, points, feat), lambda i: (i, 0, 0)),
            pl.BlockSpec((points // 4, feat), lambda i: (i, 0)),
        ],
        out_shape=[
            jax.ShapeDtypeStruct((lats, points, feat), jnp.float32),
            jax.ShapeDtypeStruct((lats // 2 * (points // 4), feat), jnp.bfloat16),
        ],
        scratch_shapes=[pltpu.VMEM((points, feat), jnp.float32)],
        name="to_grid",
        cost_estimate=cost(2 * coeffs.size * points, 2 * coeffs.size + 2 * table.size),
    )(coeffs, table)


def fourier_kernel(forced_ref, returned_ref, table_ref, out_ref, fine):
    lats, points, feat = forced_ref.shape
    devices, _, slots, _ = out_ref.shape
    coarse = returned_ref[...].astype(jnp.float32)
    count = coarse.shape[0]
    before = pltpu.roll(coarse, 1, 0)
    following = pltpu.roll(coarse, count - 1, 0)
    pieces = [
        0.375 * before + 0.625 * coarse,
        0.125 * before + 0.875 * coarse,
        0.875 * coarse + 0.125 * following,
        0.625 * coarse + 0.375 * following,
    ]
    for u, piece in enumerate(pieces):
        fine[pl.ds(u, count, stride=4), :] = piece
    correction = fine[...]
    right = jnp.concatenate(
        [(forced_ref[t] + correction).astype(jnp.bfloat16) for t in range(lats)], axis=1
    )
    waves = jnp.dot(table_ref[...], right, preferred_element_type=jnp.float32)
    half = devices * slots
    for t in range(lats):
        for r in range(2):
            part = waves[r * half : (r + 1) * half, t * feat : (t + 1) * feat]
            out_ref[:, t, :, r * feat : (r + 1) * feat] = part.reshape(devices, slots, feat).astype(
                jnp.bfloat16
            )


def to_fourier(forced, returned, table, devices):
    lats, points, feat = forced.shape
    slots = table.shape[0] // (2 * devices)
    return pl.pallas_call(
        fourier_kernel,
        grid=(lats // 2,),
        in_specs=[
            pl.BlockSpec((2, points, feat), lambda i: (i, 0, 0)),
            pl.BlockSpec((points // 4, feat), lambda i: (i, 0)),
            pl.BlockSpec(table.shape, lambda i: (0, 0)),
        ],
        out_specs=pl.BlockSpec((devices, 2, slots, 2 * feat), lambda i: (0, i, 0, 0)),
        out_shape=jax.ShapeDtypeStruct((devices, lats, slots, 2 * feat), jnp.bfloat16),
        scratch_shapes=[pltpu.VMEM((points, feat), jnp.float32)],
        name="to_fourier",
        cost_estimate=cost(2 * forced.size * table.shape[0], 4 * forced.size + 2 * table.size),
    )(forced, returned, table)


def forward_kernel(spans, low_ref, legendre_ref, order_ref, *rest):
    coeffs, out_ref, scratch = rest[:-2], rest[-2], rest[-1]
    step = pl.program_id(0)
    _, degrees, channels = out_ref.shape
    lat_total = legendre_ref.shape[1]
    rows = 2 * PAIR_STEP
    devices = coeffs[0].shape[0]
    per_device = lat_total // devices
    for ref, (first, count) in zip(coeffs, spans):
        for d in range(devices):
            block = ref[d].astype(jnp.float32).reshape(count * rows, channels)
            for h in range(channels // 128):
                scratch[h, pl.ds((d * per_device + first) * rows, count * rows), :] = block[
                    :, h * 128 : (h + 1) * 128
                ]
    degree = lax.broadcasted_iota(jnp.int32, (degrees, channels), 0)
    for i in range(PAIR_STEP):
        low = low_ref[step * PAIR_STEP + i]
        sides = []
        for s in range(2):
            side = jnp.concatenate(
                [
                    scratch[h, pl.ds(2 * i + s, lat_total, stride=rows), :]
                    for h in range(channels // 128)
                ],
                axis=1,
            ).astype(jnp.bfloat16)
            sides.append(
                lax.dot_general(
                    side,
                    order_ref[...],
                    (((1,), (1,)), ((), ())),
                    preferred_element_type=jnp.float32,
                ).astype(jnp.bfloat16)
            )
        both = lax.dot_general(
            legendre_ref[i],
            jnp.concatenate(sides, axis=1),
            (((0,), (0,)), ((), ())),
            preferred_element_type=jnp.float32,
        )
        lower = degree < degrees - 1 - low
        out_ref[i] = jnp.where(lower, both[:, :channels], both[:, channels:]).astype(jnp.bfloat16)


def forward_legendre(coeffs, legendre, local_low, order, spans):
    pair_count, lat_total, degrees = legendre.shape
    channels = order.shape[0]
    rows = 2 * PAIR_STEP
    devices = coeffs[0].shape[0]
    return pl.pallas_call(
        functools.partial(forward_kernel, spans),
        grid_spec=pltpu.PrefetchScalarGridSpec(
            num_scalar_prefetch=1,
            grid=(pair_count // PAIR_STEP,),
            in_specs=[
                pl.BlockSpec((PAIR_STEP, lat_total, degrees), lambda g, low: (g, 0, 0)),
                pl.BlockSpec((channels, channels), lambda g, low: (0, 0)),
            ]
            + [
                pl.BlockSpec((devices, count, rows, channels), lambda g, low: (0, 0, g, 0))
                for _, count in spans
            ],
            out_specs=pl.BlockSpec((PAIR_STEP, degrees, channels), lambda g, low: (g, 0, 0)),
            scratch_shapes=[pltpu.VMEM((channels // 128, lat_total * rows, 128), jnp.float32)],
        ),
        out_shape=jax.ShapeDtypeStruct((pair_count, degrees, channels), jnp.bfloat16),
        name="forward_legendre",
        cost_estimate=cost(
            4 * pair_count * degrees * lat_total * channels, 4 * legendre.size
        ),
    )(local_low, legendre, order, *coeffs)


def smooth(values):
    half = 0.5 * values
    return half + half * jnp.tanh(half)


def network_kernel(
    sent_ref, in_ref, mid_ref, out_ref, result_ref, arrived, answers, sends, arrivals, backs, returns
):
    devices = sent_ref.shape[0]
    me = lax.axis_index("wave")
    barrier = pltpu.get_barrier_semaphore()

    def peer(k):
        return lax.rem(me + k, devices)

    def outward(k, source, target):
        return pltpu.make_async_remote_copy(
            src_ref=sent_ref.at[target],
            dst_ref=arrived.at[source],
            send_sem=sends.at[k],
            recv_sem=arrivals.at[k],
            device_id={"wave": peer(k)},
            device_id_type=pl.DeviceIdType.MESH,
        )

    def backward(k, source, owner):
        return pltpu.make_async_remote_copy(
            src_ref=answers.at[source],
            dst_ref=result_ref.at[owner],
            send_sem=backs.at[k],
            recv_sem=returns.at[k],
            device_id={"wave": peer(devices - k)},
            device_id_type=pl.DeviceIdType.MESH,
        )

    def answer(rows):
        hidden = smooth(jnp.dot(rows, in_ref[0], preferred_element_type=jnp.float32))
        deeper = smooth(
            jnp.dot(hidden.astype(jnp.bfloat16), mid_ref[0], preferred_element_type=jnp.float32)
        )
        return jnp.dot(
            deeper.astype(jnp.bfloat16), out_ref[0], preferred_element_type=jnp.float32
        ).astype(jnp.bfloat16)

    def greet(k, carry):
        pl.semaphore_signal(
            barrier, inc=1, device_id={"wave": peer(k)}, device_id_type=pl.DeviceIdType.MESH
        )
        return carry

    def send(k, carry):
        outward(k, me, peer(k)).start()
        return carry

    def serve(k, carry):
        source = peer(devices - k)
        outward(k, source, peer(k)).wait_recv()
        answers[source] = answer(arrived[source])
        backward(k, source, me).start()
        return carry

    def finish(k, carry):
        outward(k, me, peer(k)).wait_send()
        backward(k, peer(devices - k), me).wait_send()
        backward(k, peer(k), peer(k)).wait_recv()
        return carry

    lax.fori_loop(1, devices, greet, 0)
    pl.semaphore_wait(barrier, devices - 1)
    lax.fori_loop(1, devices, send, 0)
    result_ref[me] = answer(sent_ref[me])
    lax.fori_loop(1, devices, serve, 0)
    lax.fori_loop(1, devices, finish, 0)


def run_network(outgoing, w_in, w_mid, w_out):
    devices, slots, feat = outgoing.shape
    return pl.pallas_call(
        network_kernel,
        in_specs=[pl.BlockSpec(memory_space=pltpu.VMEM)] * 4,
        out_specs=pl.BlockSpec(memory_space=pltpu.VMEM),
        out_shape=jax.ShapeDtypeStruct(outgoing.shape, jnp.bfloat16),
        scratch_shapes=[pltpu.VMEM(outgoing.shape, jnp.bfloat16)] * 2
        + [pltpu.SemaphoreType.DMA((devices,))] * 4,
        compiler_params=pltpu.CompilerParams(collective_id=0, has_side_effects=True),
        name="network",
        cost_estimate=cost(
            2 * devices * slots * (w_in.size + w_mid.size + w_out.size),
            4 * outgoing.size + 2 * w_mid.size,
        ),
    )(outgoing, w_in, w_mid, w_out)


def phase_tables(wavenums, points):
    longitude = jnp.arange(points, dtype=jnp.int32)
    turn = jnp.float32(2.0 * math.pi / points)
    angles = (wavenums[:, None] * longitude[None, :] % points).astype(jnp.float32) * turn
    scale = jnp.float32(1.0 / math.sqrt(points))
    forward = jnp.concatenate([scale * jnp.cos(angles), -scale * jnp.sin(angles)], axis=0).astype(
        jnp.bfloat16
    )
    angles = (longitude[:, None] * wavenums[None, :] % points).astype(jnp.float32) * turn
    factor = jnp.where(wavenums == 0, jnp.float32(1.0), jnp.float32(2.0))[None, :]
    inverse = jnp.concatenate([factor * jnp.cos(angles), -factor * jnp.sin(angles)], axis=1).astype(
        jnp.bfloat16
    )
    return inverse, forward


def exchange(values):
    return lax.all_to_all(values, "wave", split_axis=0, concat_axis=0, tiled=True)


def row_spans(lat_rows):
    pairs = lat_rows // 2
    first = max(1, pairs * 4 // 5)
    spans = [(0, 2 * first), (2 * first, 2 * (pairs - first))]
    return [span for span in spans if span[1] > 0]


def on_device_kernels(spectral, legendre, pair_low, routes, w_in, w_mid, w_out):
    pair_count, degrees, channels = spectral.shape
    feat = channels // 2
    lat_total = legendre.shape[2]
    wave_total = degrees - 1
    devices = lax.axis_size("wave")
    lat_rows = lat_total // devices
    spans = row_spans(lat_rows)
    local_low = lax.dynamic_slice_in_dim(pair_low, lax.axis_index("wave") * pair_count, pair_count)
    order = channel_order(channels)
    turned = jnp.swapaxes(legendre, 1, 2)
    sent = inverse_legendre(spectral, turned, local_low, order, spans, devices)
    pair_low, routes, *sent = lax.optimization_barrier((pair_low, routes, *sent))
    arriving = exchange(sent[0])
    inverse_table, forward_table = phase_tables(slot_waves(pair_low, wave_total), NLON)
    regimes = routes[:, 0]
    total_columns = regimes.shape[0]
    positions = slot_positions(regimes.reshape(1, -1), devices)[0]
    capacity = 2 * total_columns // devices
    places = regimes * capacity + positions
    outgoing = jnp.zeros((devices * capacity, feat), jnp.bfloat16)
    forced = []
    width = NLON // 4
    for part, (first, count) in enumerate(spans):
        held = (arriving, sent[part + 1 :], inverse_table, forward_table, places, outgoing)
        arriving, later, inverse_table, forward_table, places, outgoing = lax.optimization_barrier(
            held
        )
        arrived = arriving
        if later:
            sent[part + 1 :] = later
            arriving = exchange(sent[part + 1])
        forced_part, columns = to_grid(arrived, inverse_table)
        forced.append(forced_part)
        at = places[first // 2 * width : (first + count) // 2 * width]
        outgoing = outgoing.at[at].set(columns, unique_indices=True, mode="promise_in_bounds")
    incoming = run_network(outgoing.reshape(devices, capacity, feat), w_in, w_mid, w_out)
    incoming = incoming.reshape(-1, feat)
    received = [None] * len(spans)
    for part in reversed(range(len(spans))):
        first, count = spans[part]
        at = places[first // 2 * width : (first + count) // 2 * width]
        returned = incoming.at[at].get(mode="promise_in_bounds")
        received[part] = exchange(to_fourier(forced[part], returned, forward_table, devices))
    return forward_legendre(received, turned, local_low, order, spans)


def on_device(spectral, legendre, pair_low, routes, w_in, w_mid, w_out):
    devices = lax.axis_size("wave")
    aligned = (
        spectral.shape[0] % PAIR_STEP == 0
        and 2 * spectral.shape[0] % 8 == 0
        and legendre.shape[2] // devices % 2 == 0
        and 2 * routes.shape[0] // devices % 8 == 0
    )
    body = on_device_kernels if aligned else on_device_arrays
    return body(spectral, legendre, pair_low, routes, w_in, w_mid, w_out)


def solution(mesh):
    placed = (
        P(("grp", "wave"), None, None),
        P("wave", None, None),
        P(),
        P(("grp", "wave"), None),
        P("wave", None, None),
        P("wave", None, None),
        P("wave", None, None),
    )
    return jax.shard_map(
        on_device,
        mesh=mesh,
        in_specs=placed,
        out_specs=P(("grp", "wave"), None, None),
        check_vma=False,
    )
```

```python
import functools
import math

import jax
import jax.numpy as jnp
from jax import lax
from jax.experimental import pallas as pl
from jax.experimental.pallas import tpu as pltpu
from jax.sharding import PartitionSpec as P

NLON = 1280
FIELDS = 4
PAIR_STEP = 4


def slot_waves(pair_low, wave_total):
    return jnp.stack([pair_low, wave_total - 1 - pair_low], axis=1).reshape(-1)


def side_masks(pair_low, wave_total):
    degree = jnp.arange(wave_total + 1, dtype=jnp.int32)
    lower_side = degree[None, :] < (wave_total - pair_low)[:, None]
    return jnp.stack([lower_side, jnp.logical_not(lower_side)], axis=1)


def fourier_table(wavenums, points, inverse):
    longitude = jnp.arange(points, dtype=jnp.int32)
    phases = wavenums[:, None] * longitude[None, :] % points
    angles = phases.astype(jnp.float32) * jnp.float32(2.0 * math.pi / points)
    if inverse:
        factor = jnp.where(wavenums == 0, jnp.float32(1.0), jnp.float32(2.0))[:, None]
    else:
        factor = jnp.full((wavenums.shape[0], 1), 1.0 / math.sqrt(points), jnp.float32)
    return jnp.stack([factor * jnp.cos(angles), -factor * jnp.sin(angles)], axis=1).astype(
        jnp.bfloat16
    )


def forcing(grid_fields):
    flattened = grid_fields.reshape(FIELDS, -1)
    return (flattened * jnp.roll(flattened, -1, axis=0)).reshape(grid_fields.shape)


def coarse_columns(grid_fields):
    feat_width = grid_fields.shape[0]
    lat_rows = grid_fields.shape[1]
    lon_count = grid_fields.shape[2]
    blocks = grid_fields.reshape(feat_width, lat_rows // 2, 2, lon_count // 4, 4).mean(axis=(2, 4))
    return blocks.reshape(feat_width, -1).T.astype(jnp.bfloat16)


def spread_back(values, lat_rows):
    feat_width = values.shape[1]
    coarse = values.astype(jnp.float32).T.reshape(feat_width, lat_rows // 2, -1)
    before = jnp.roll(coarse, 1, axis=2)
    following = jnp.roll(coarse, -1, axis=2)
    pieces = [
        0.375 * before + 0.625 * coarse,
        0.125 * before + 0.875 * coarse,
        0.875 * coarse + 0.125 * following,
        0.625 * coarse + 0.375 * following,
    ]
    fine_grid = jnp.stack(pieces, axis=3).reshape(feat_width, lat_rows // 2, -1)
    return jnp.repeat(fine_grid, 2, axis=1)


def slot_positions(regimes, experts_total):
    onehot = (regimes[:, :, None] == jnp.arange(experts_total, dtype=jnp.int32)).astype(jnp.int32)
    ranking = jnp.cumsum(onehot, axis=1) - 1
    return jnp.sum(ranking * onehot, axis=2)


def network(columns, weight_in, weight_mid, weight_out):
    hidden = jax.nn.silu(jnp.dot(columns, weight_in, preferred_element_type=jnp.float32)).astype(
        jnp.bfloat16
    )
    deeper = jax.nn.silu(jnp.dot(hidden, weight_mid, preferred_element_type=jnp.float32)).astype(
        jnp.bfloat16
    )
    return jnp.dot(deeper, weight_out, preferred_element_type=jnp.float32).astype(jnp.bfloat16)


def masked_inverse(spectral, legendre, side_mask):
    masked = jnp.where(side_mask[:, :, :, None], spectral[:, None], jnp.zeros((), jnp.bfloat16))
    return jnp.einsum("psjc,pjl->pscl", masked, legendre, preferred_element_type=jnp.float32)


def masked_forward(legendre, coeffs, side_mask):
    both_sides = jnp.einsum(
        "pjl,pskrl->psjkr", legendre, coeffs, preferred_element_type=jnp.float32
    )
    return jnp.sum(jnp.where(side_mask[:, :, :, None, None], both_sides, 0.0), axis=1)


def on_device_arrays(spectral, legendre, pair_low, routes, w_in, w_mid, w_out):
    pair_count = spectral.shape[0]
    degrees = spectral.shape[1]
    channels = spectral.shape[2]
    feat_width = channels // 2
    lat_total = legendre.shape[2]
    wave_total = degrees - 1
    devices = lax.axis_size("wave")
    local_low = lax.dynamic_slice_in_dim(pair_low, lax.axis_index("wave") * pair_count, pair_count)
    side_mask = side_masks(local_low, wave_total)
    inverse_out = masked_inverse(spectral, legendre, side_mask)
    fourier_in = inverse_out.astype(jnp.bfloat16).reshape(2 * pair_count, feat_width, 2, lat_total)
    wavenums = slot_waves(pair_low, wave_total)
    inverse_table = fourier_table(wavenums, NLON, True)
    grid_fields = jnp.einsum(
        "qkra,qrl->kal",
        lax.all_to_all(fourier_in, "wave", split_axis=3, concat_axis=0, tiled=True),
        inverse_table,
        preferred_element_type=jnp.float32,
    )
    lat_rows = grid_fields.shape[1]
    forced = forcing(grid_fields)
    columns = coarse_columns(grid_fields)
    regimes = routes[:, 0].reshape(1, -1)
    positions = slot_positions(regimes, devices)[0]
    regime_row = regimes[0]
    capacity = 2 * columns.shape[0] // devices
    outgoing = (
        jnp.zeros((devices, capacity, feat_width), jnp.bfloat16)
        .at[regime_row, positions]
        .set(columns)
    )
    arrived = lax.all_to_all(outgoing, "wave", split_axis=0, concat_axis=0, tiled=True)
    answers = network(arrived.reshape(-1, feat_width), w_in[0], w_mid[0], w_out[0]).reshape(
        arrived.shape
    )
    incoming = lax.all_to_all(answers, "wave", split_axis=0, concat_axis=0, tiled=True)
    returned = incoming[regime_row, positions]
    correction = spread_back(returned, lat_rows)
    tendency_grid = (forced + correction).astype(jnp.bfloat16)
    forward_table = fourier_table(wavenums, NLON, False)
    fourier_out = jnp.einsum(
        "fal,qrl->qfra", tendency_grid, forward_table, preferred_element_type=jnp.float32
    ).astype(jnp.bfloat16)
    received = lax.all_to_all(fourier_out, "wave", split_axis=0, concat_axis=3, tiled=True)
    coeffs = received.reshape(pair_count, 2, received.shape[1], 2, received.shape[3])
    result = masked_forward(legendre, coeffs, side_mask)
    spectral_out = result.astype(jnp.bfloat16)
    return spectral_out.reshape(pair_count, degrees, channels)


def cost(flops, moved):
    return pl.CostEstimate(flops=int(flops), bytes_accessed=int(moved), transcendentals=0)


def channel_order(channels):
    source = jnp.arange(channels, dtype=jnp.int32)
    target = source % 2 * (channels // 2) + source // 2
    return (target[:, None] == source[None, :]).astype(jnp.bfloat16)


def inverse_kernel(spans, devices, low_ref, spectral_ref, legendre_ref, order_ref, *rest):
    outs, scratch = rest[:-1], rest[-1]
    step = pl.program_id(0)
    degrees, channels = spectral_ref.shape[1:]
    lat_total = legendre_ref.shape[1]
    rows = 2 * PAIR_STEP
    degree = lax.broadcasted_iota(jnp.int32, (degrees, channels), 0)
    for i in range(PAIR_STEP):
        low = low_ref[step * PAIR_STEP + i]
        ordered = jnp.dot(spectral_ref[i], order_ref[...], preferred_element_type=jnp.float32)
        lower = degree < degrees - 1 - low
        sides = jnp.concatenate(
            [jnp.where(lower, ordered, 0.0), jnp.where(lower, 0.0, ordered)], axis=1
        ).astype(jnp.bfloat16)
        result = jnp.dot(legendre_ref[i], sides, preferred_element_type=jnp.float32)
        for s in range(2):
            for h in range(channels // 128):
                at = s * channels + h * 128
                scratch[h, pl.ds(2 * i + s, lat_total, stride=rows), :] = result[:, at : at + 128]
    per_device = lat_total // devices
    for out, (first, count) in zip(outs, spans):
        for d in range(devices):
            for h in range(channels // 128):
                block = scratch[h, pl.ds((d * per_device + first) * rows, count * rows), :]
                out[d, :, :, h * 128 : (h + 1) * 128] = block.reshape(count, rows, 128).astype(
                    jnp.bfloat16
                )


def inverse_legendre(spectral, legendre, local_low, order, spans, devices):
    pair_count, degrees, channels = spectral.shape
    lat_total = legendre.shape[1]
    rows = 2 * PAIR_STEP
    return pl.pallas_call(
        functools.partial(inverse_kernel, spans, devices),
        grid_spec=pltpu.PrefetchScalarGridSpec(
            num_scalar_prefetch=1,
            grid=(pair_count // PAIR_STEP,),
            in_specs=[
                pl.BlockSpec((PAIR_STEP, degrees, channels), lambda g, low: (g, 0, 0)),
                pl.BlockSpec((PAIR_STEP, lat_total, degrees), lambda g, low: (g, 0, 0)),
                pl.BlockSpec((channels, channels), lambda g, low: (0, 0)),
            ],
            out_specs=[
                pl.BlockSpec((devices, count, rows, channels), lambda g, low: (0, 0, g, 0))
                for _, count in spans
            ],
            scratch_shapes=[pltpu.VMEM((channels // 128, lat_total * rows, 128), jnp.float32)],
        ),
        out_shape=[
            jax.ShapeDtypeStruct((devices, count, 2 * pair_count, channels), jnp.bfloat16)
            for _, count in spans
        ],
        name="inverse_legendre",
        cost_estimate=cost(
            4 * pair_count * degrees * lat_total * channels, 2 * spectral.size * 2 + 2 * legendre.size
        ),
    )(local_low, spectral, legendre, order)


def grid_kernel(coeff_ref, table_ref, forced_ref, columns_ref, pooled):
    devices, lats, slots, channels = coeff_ref.shape
    feat = channels // 2
    rights = []
    for t in range(lats):
        waves = coeff_ref[:, t].astype(jnp.float32).reshape(devices * slots, channels)
        rights.append(
            jnp.concatenate([waves[:, :feat], waves[:, feat:]], axis=0).astype(jnp.bfloat16)
        )
    fields = jnp.dot(
        table_ref[...], jnp.concatenate(rights, axis=1), preferred_element_type=jnp.float32
    )
    total = None
    for t in range(lats):
        one = fields[:, t * feat : (t + 1) * feat]
        forced_ref[t] = one * pltpu.roll(one, feat - feat // 4, 1)
        total = one if total is None else total + one
    pooled[...] = total
    count = columns_ref.shape[0]
    spread = total.shape[0] // count
    mean = pooled[pl.ds(0, count, stride=spread), :]
    for u in range(1, spread):
        mean = mean + pooled[pl.ds(u, count, stride=spread), :]
    columns_ref[...] = (mean * (1.0 / (spread * lats))).astype(jnp.bfloat16)


def to_grid(coeffs, table):
    devices, lats, slots, channels = coeffs.shape
    points = table.shape[0]
    feat = channels // 2
    return pl.pallas_call(
        grid_kernel,
        grid=(lats // 2,),
        in_specs=[
            pl.BlockSpec((devices, 2, slots, channels), lambda i: (0, i, 0, 0)),
            pl.BlockSpec(table.shape, lambda i: (0, 0)),
        ],
        out_specs=[
            pl.BlockSpec((2, points, feat), lambda i: (i, 0, 0)),
            pl.BlockSpec((points // 4, feat), lambda i: (i, 0)),
        ],
        out_shape=[
            jax.ShapeDtypeStruct((lats, points, feat), jnp.float32),
            jax.ShapeDtypeStruct((lats // 2 * (points // 4), feat), jnp.bfloat16),
        ],
        scratch_shapes=[pltpu.VMEM((points, feat), jnp.float32)],
        name="to_grid",
        cost_estimate=cost(2 * coeffs.size * points, 2 * coeffs.size + 2 * table.size),
    )(coeffs, table)


def fourier_kernel(forced_ref, returned_ref, table_ref, out_ref, fine):
    lats, points, feat = forced_ref.shape
    devices, _, slots, _ = out_ref.shape
    coarse = returned_ref[...].astype(jnp.float32)
    count = coarse.shape[0]
    before = pltpu.roll(coarse, 1, 0)
    following = pltpu.roll(coarse, count - 1, 0)
    pieces = [
        0.375 * before + 0.625 * coarse,
        0.125 * before + 0.875 * coarse,
        0.875 * coarse + 0.125 * following,
        0.625 * coarse + 0.375 * following,
    ]
    for u, piece in enumerate(pieces):
        fine[pl.ds(u, count, stride=4), :] = piece
    correction = fine[...]
    right = jnp.concatenate(
        [(forced_ref[t] + correction).astype(jnp.bfloat16) for t in range(lats)], axis=1
    )
    waves = jnp.dot(table_ref[...], right, preferred_element_type=jnp.float32)
    half = devices * slots
    for t in range(lats):
        for r in range(2):
            part = waves[r * half : (r + 1) * half, t * feat : (t + 1) * feat]
            out_ref[:, t, :, r * feat : (r + 1) * feat] = part.reshape(devices, slots, feat).astype(
                jnp.bfloat16
            )


def to_fourier(forced, returned, table, devices):
    lats, points, feat = forced.shape
    slots = table.shape[0] // (2 * devices)
    return pl.pallas_call(
        fourier_kernel,
        grid=(lats // 2,),
        in_specs=[
            pl.BlockSpec((2, points, feat), lambda i: (i, 0, 0)),
            pl.BlockSpec((points // 4, feat), lambda i: (i, 0)),
            pl.BlockSpec(table.shape, lambda i: (0, 0)),
        ],
        out_specs=pl.BlockSpec((devices, 2, slots, 2 * feat), lambda i: (0, i, 0, 0)),
        out_shape=jax.ShapeDtypeStruct((devices, lats, slots, 2 * feat), jnp.bfloat16),
        scratch_shapes=[pltpu.VMEM((points, feat), jnp.float32)],
        name="to_fourier",
        cost_estimate=cost(2 * forced.size * table.shape[0], 4 * forced.size + 2 * table.size),
    )(forced, returned, table)


def forward_kernel(spans, low_ref, legendre_ref, order_ref, *rest):
    coeffs, out_ref, scratch = rest[:-2], rest[-2], rest[-1]
    step = pl.program_id(0)
    _, degrees, channels = out_ref.shape
    lat_total = legendre_ref.shape[1]
    rows = 2 * PAIR_STEP
    devices = coeffs[0].shape[0]
    per_device = lat_total // devices
    for ref, (first, count) in zip(coeffs, spans):
        for d in range(devices):
            block = ref[d].astype(jnp.float32).reshape(count * rows, channels)
            for h in range(channels // 128):
                scratch[h, pl.ds((d * per_device + first) * rows, count * rows), :] = block[
                    :, h * 128 : (h + 1) * 128
                ]
    degree = lax.broadcasted_iota(jnp.int32, (degrees, channels), 0)
    for i in range(PAIR_STEP):
        low = low_ref[step * PAIR_STEP + i]
        sides = []
        for s in range(2):
            side = jnp.concatenate(
                [
                    scratch[h, pl.ds(2 * i + s, lat_total, stride=rows), :]
                    for h in range(channels // 128)
                ],
                axis=1,
            ).astype(jnp.bfloat16)
            sides.append(
                lax.dot_general(
                    side,
                    order_ref[...],
                    (((1,), (1,)), ((), ())),
                    preferred_element_type=jnp.float32,
                ).astype(jnp.bfloat16)
            )
        both = lax.dot_general(
            legendre_ref[i],
            jnp.concatenate(sides, axis=1),
            (((0,), (0,)), ((), ())),
            preferred_element_type=jnp.float32,
        )
        lower = degree < degrees - 1 - low
        out_ref[i] = jnp.where(lower, both[:, :channels], both[:, channels:]).astype(jnp.bfloat16)


def forward_legendre(coeffs, legendre, local_low, order, spans):
    pair_count, lat_total, degrees = legendre.shape
    channels = order.shape[0]
    rows = 2 * PAIR_STEP
    devices = coeffs[0].shape[0]
    return pl.pallas_call(
        functools.partial(forward_kernel, spans),
        grid_spec=pltpu.PrefetchScalarGridSpec(
            num_scalar_prefetch=1,
            grid=(pair_count // PAIR_STEP,),
            in_specs=[
                pl.BlockSpec((PAIR_STEP, lat_total, degrees), lambda g, low: (g, 0, 0)),
                pl.BlockSpec((channels, channels), lambda g, low: (0, 0)),
            ]
            + [
                pl.BlockSpec((devices, count, rows, channels), lambda g, low: (0, 0, g, 0))
                for _, count in spans
            ],
            out_specs=pl.BlockSpec((PAIR_STEP, degrees, channels), lambda g, low: (g, 0, 0)),
            scratch_shapes=[pltpu.VMEM((channels // 128, lat_total * rows, 128), jnp.float32)],
        ),
        out_shape=jax.ShapeDtypeStruct((pair_count, degrees, channels), jnp.bfloat16),
        name="forward_legendre",
        cost_estimate=cost(
            4 * pair_count * degrees * lat_total * channels, 4 * legendre.size
        ),
    )(local_low, legendre, order, *coeffs)


def smooth(values):
    half = 0.5 * values
    return half + half * jnp.tanh(half)


def network_kernel(
    sent_ref, in_ref, mid_ref, out_ref, result_ref, arrived, answers, sends, arrivals, backs, returns
):
    devices = sent_ref.shape[0]
    me = lax.axis_index("wave")
    barrier = pltpu.get_barrier_semaphore()

    def peer(k):
        other = 0
        for bit in range(devices.bit_length() - 1):
            other = other + (me // (1 << bit) + k // (1 << bit)) % 2 * (1 << bit)
        return other

    def outward(k, source, target):
        return pltpu.make_async_remote_copy(
            src_ref=sent_ref.at[target],
            dst_ref=arrived.at[source],
            send_sem=sends.at[k],
            recv_sem=arrivals.at[k],
            device_id={"wave": peer(k)},
            device_id_type=pl.DeviceIdType.MESH,
        )

    def backward(k, source, owner):
        return pltpu.make_async_remote_copy(
            src_ref=answers.at[source],
            dst_ref=result_ref.at[owner],
            send_sem=backs.at[k],
            recv_sem=returns.at[k],
            device_id={"wave": peer(k)},
            device_id_type=pl.DeviceIdType.MESH,
        )

    def answer(rows):
        hidden = smooth(jnp.dot(rows, in_ref[0], preferred_element_type=jnp.float32))
        deeper = smooth(
            jnp.dot(hidden.astype(jnp.bfloat16), mid_ref[0], preferred_element_type=jnp.float32)
        )
        return jnp.dot(
            deeper.astype(jnp.bfloat16), out_ref[0], preferred_element_type=jnp.float32
        ).astype(jnp.bfloat16)

    def greet(k, carry):
        pl.semaphore_signal(
            barrier, inc=1, device_id={"wave": peer(k)}, device_id_type=pl.DeviceIdType.MESH
        )
        return carry

    def send(i, carry):
        k = devices - i
        outward(k, me, peer(k)).start()
        return carry

    def serve(i, carry):
        k = devices - i
        source = peer(k)
        outward(k, source, peer(k)).wait_recv()
        answers[source] = answer(arrived[source])
        backward(k, source, me).start()
        return carry

    def finish(k, carry):
        outward(k, me, peer(k)).wait_send()
        backward(k, peer(k), me).wait_send()
        backward(k, peer(k), peer(k)).wait_recv()
        return carry

    lax.fori_loop(1, devices, greet, 0)
    pl.semaphore_wait(barrier, devices - 1)
    lax.fori_loop(1, devices, send, 0)
    result_ref[me] = answer(sent_ref[me])
    lax.fori_loop(1, devices, serve, 0)
    lax.fori_loop(1, devices, finish, 0)


def run_network(outgoing, w_in, w_mid, w_out):
    devices, slots, feat = outgoing.shape
    return pl.pallas_call(
        network_kernel,
        in_specs=[pl.BlockSpec(memory_space=pltpu.VMEM)] * 4,
        out_specs=pl.BlockSpec(memory_space=pltpu.VMEM),
        out_shape=jax.ShapeDtypeStruct(outgoing.shape, jnp.bfloat16),
        scratch_shapes=[pltpu.VMEM(outgoing.shape, jnp.bfloat16)] * 2
        + [pltpu.SemaphoreType.DMA((devices,))] * 4,
        compiler_params=pltpu.CompilerParams(collective_id=0, has_side_effects=True),
        name="network",
        cost_estimate=cost(
            2 * devices * slots * (w_in.size + w_mid.size + w_out.size),
            4 * outgoing.size + 2 * w_mid.size,
        ),
    )(outgoing, w_in, w_mid, w_out)


def phase_tables(wavenums, points):
    longitude = jnp.arange(points, dtype=jnp.int32)
    turn = jnp.float32(2.0 * math.pi / points)
    angles = (wavenums[:, None] * longitude[None, :] % points).astype(jnp.float32) * turn
    scale = jnp.float32(1.0 / math.sqrt(points))
    forward = jnp.concatenate([scale * jnp.cos(angles), -scale * jnp.sin(angles)], axis=0).astype(
        jnp.bfloat16
    )
    angles = (longitude[:, None] * wavenums[None, :] % points).astype(jnp.float32) * turn
    factor = jnp.where(wavenums == 0, jnp.float32(1.0), jnp.float32(2.0))[None, :]
    inverse = jnp.concatenate([factor * jnp.cos(angles), -factor * jnp.sin(angles)], axis=1).astype(
        jnp.bfloat16
    )
    return inverse, forward


def exchange(values):
    return lax.all_to_all(values, "wave", split_axis=0, concat_axis=0, tiled=True)


def row_spans(lat_rows):
    pairs = lat_rows // 2
    first = max(1, pairs * 4 // 5)
    spans = [(0, 2 * first), (2 * first, 2 * (pairs - first))]
    return [span for span in spans if span[1] > 0]


def on_device_kernels(spectral, legendre, pair_low, routes, w_in, w_mid, w_out):
    pair_count, degrees, channels = spectral.shape
    feat = channels // 2
    lat_total = legendre.shape[2]
    wave_total = degrees - 1
    devices = lax.axis_size("wave")
    lat_rows = lat_total // devices
    spans = row_spans(lat_rows)
    local_low = lax.dynamic_slice_in_dim(pair_low, lax.axis_index("wave") * pair_count, pair_count)
    order = channel_order(channels)
    turned = jnp.swapaxes(legendre, 1, 2)
    sent = inverse_legendre(spectral, turned, local_low, order, spans, devices)
    pair_low, routes, *sent = lax.optimization_barrier((pair_low, routes, *sent))
    arriving = exchange(sent[0])
    inverse_table, forward_table = phase_tables(slot_waves(pair_low, wave_total), NLON)
    regimes = routes[:, 0]
    total_columns = regimes.shape[0]
    positions = slot_positions(regimes.reshape(1, -1), devices)[0]
    capacity = 2 * total_columns // devices
    places = regimes * capacity + positions
    outgoing = jnp.zeros((devices * capacity, feat), jnp.bfloat16)
    forced = []
    width = NLON // 4
    for part, (first, count) in enumerate(spans):
        held = (arriving, sent[part + 1 :], inverse_table, forward_table, places, outgoing)
        arriving, later, inverse_table, forward_table, places, outgoing = lax.optimization_barrier(
            held
        )
        arrived = arriving
        if later:
            sent[part + 1 :] = later
            arriving = exchange(sent[part + 1])
        forced_part, columns = to_grid(arrived, inverse_table)
        forced.append(forced_part)
        at = places[first // 2 * width : (first + count) // 2 * width]
        outgoing = outgoing.at[at].set(columns, unique_indices=True, mode="promise_in_bounds")
    incoming = run_network(outgoing.reshape(devices, capacity, feat), w_in, w_mid, w_out)
    incoming = incoming.reshape(-1, feat)
    received = [None] * len(spans)
    for part in reversed(range(len(spans))):
        first, count = spans[part]
        at = places[first // 2 * width : (first + count) // 2 * width]
        returned = incoming.at[at].get(mode="promise_in_bounds")
        received[part] = exchange(to_fourier(forced[part], returned, forward_table, devices))
    return forward_legendre(received, turned, local_low, order, spans)


def on_device(spectral, legendre, pair_low, routes, w_in, w_mid, w_out):
    devices = lax.axis_size("wave")
    aligned = (
        spectral.shape[0] % PAIR_STEP == 0
        and 2 * spectral.shape[0] % 8 == 0
        and legendre.shape[2] // devices % 2 == 0
        and 2 * routes.shape[0] // devices % 8 == 0
        and devices & (devices - 1) == 0
    )
    body = on_device_kernels if aligned else on_device_arrays
    return body(spectral, legendre, pair_low, routes, w_in, w_mid, w_out)


def solution(mesh):
    placed = (
        P(("grp", "wave"), None, None),
        P("wave", None, None),
        P(),
        P(("grp", "wave"), None),
        P("wave", None, None),
        P("wave", None, None),
        P("wave", None, None),
    )
    return jax.shard_map(
        on_device,
        mesh=mesh,
        in_specs=placed,
        out_specs=P(("grp", "wave"), None, None),
        check_vma=False,
    )
```

```python
import functools
import math

import jax
import jax.numpy as jnp
from jax import lax
from jax.experimental import pallas as pl
from jax.experimental.pallas import tpu as pltpu
from jax.sharding import PartitionSpec as P

NLON = 1280
FIELDS = 4
PAIR_STEP = 4


def slot_waves(pair_low, wave_total):
    return jnp.stack([pair_low, wave_total - 1 - pair_low], axis=1).reshape(-1)


def side_masks(pair_low, wave_total):
    degree = jnp.arange(wave_total + 1, dtype=jnp.int32)
    lower_side = degree[None, :] < (wave_total - pair_low)[:, None]
    return jnp.stack([lower_side, jnp.logical_not(lower_side)], axis=1)


def fourier_table(wavenums, points, inverse):
    longitude = jnp.arange(points, dtype=jnp.int32)
    phases = wavenums[:, None] * longitude[None, :] % points
    angles = phases.astype(jnp.float32) * jnp.float32(2.0 * math.pi / points)
    if inverse:
        factor = jnp.where(wavenums == 0, jnp.float32(1.0), jnp.float32(2.0))[:, None]
    else:
        factor = jnp.full((wavenums.shape[0], 1), 1.0 / math.sqrt(points), jnp.float32)
    return jnp.stack([factor * jnp.cos(angles), -factor * jnp.sin(angles)], axis=1).astype(
        jnp.bfloat16
    )


def forcing(grid_fields):
    flattened = grid_fields.reshape(FIELDS, -1)
    return (flattened * jnp.roll(flattened, -1, axis=0)).reshape(grid_fields.shape)


def coarse_columns(grid_fields):
    feat_width = grid_fields.shape[0]
    lat_rows = grid_fields.shape[1]
    lon_count = grid_fields.shape[2]
    blocks = grid_fields.reshape(feat_width, lat_rows // 2, 2, lon_count // 4, 4).mean(axis=(2, 4))
    return blocks.reshape(feat_width, -1).T.astype(jnp.bfloat16)


def spread_back(values, lat_rows):
    feat_width = values.shape[1]
    coarse = values.astype(jnp.float32).T.reshape(feat_width, lat_rows // 2, -1)
    before = jnp.roll(coarse, 1, axis=2)
    following = jnp.roll(coarse, -1, axis=2)
    pieces = [
        0.375 * before + 0.625 * coarse,
        0.125 * before + 0.875 * coarse,
        0.875 * coarse + 0.125 * following,
        0.625 * coarse + 0.375 * following,
    ]
    fine_grid = jnp.stack(pieces, axis=3).reshape(feat_width, lat_rows // 2, -1)
    return jnp.repeat(fine_grid, 2, axis=1)


def slot_positions(regimes, experts_total):
    onehot = (regimes[:, :, None] == jnp.arange(experts_total, dtype=jnp.int32)).astype(jnp.int32)
    ranking = jnp.cumsum(onehot, axis=1) - 1
    return jnp.sum(ranking * onehot, axis=2)


def network(columns, weight_in, weight_mid, weight_out):
    hidden = jax.nn.silu(jnp.dot(columns, weight_in, preferred_element_type=jnp.float32)).astype(
        jnp.bfloat16
    )
    deeper = jax.nn.silu(jnp.dot(hidden, weight_mid, preferred_element_type=jnp.float32)).astype(
        jnp.bfloat16
    )
    return jnp.dot(deeper, weight_out, preferred_element_type=jnp.float32).astype(jnp.bfloat16)


def masked_inverse(spectral, legendre, side_mask):
    masked = jnp.where(side_mask[:, :, :, None], spectral[:, None], jnp.zeros((), jnp.bfloat16))
    return jnp.einsum("psjc,pjl->pscl", masked, legendre, preferred_element_type=jnp.float32)


def masked_forward(legendre, coeffs, side_mask):
    both_sides = jnp.einsum(
        "pjl,pskrl->psjkr", legendre, coeffs, preferred_element_type=jnp.float32
    )
    return jnp.sum(jnp.where(side_mask[:, :, :, None, None], both_sides, 0.0), axis=1)


def on_device_arrays(spectral, legendre, pair_low, routes, w_in, w_mid, w_out):
    pair_count = spectral.shape[0]
    degrees = spectral.shape[1]
    channels = spectral.shape[2]
    feat_width = channels // 2
    lat_total = legendre.shape[2]
    wave_total = degrees - 1
    devices = lax.axis_size("wave")
    local_low = lax.dynamic_slice_in_dim(pair_low, lax.axis_index("wave") * pair_count, pair_count)
    side_mask = side_masks(local_low, wave_total)
    inverse_out = masked_inverse(spectral, legendre, side_mask)
    fourier_in = inverse_out.astype(jnp.bfloat16).reshape(2 * pair_count, feat_width, 2, lat_total)
    wavenums = slot_waves(pair_low, wave_total)
    inverse_table = fourier_table(wavenums, NLON, True)
    grid_fields = jnp.einsum(
        "qkra,qrl->kal",
        lax.all_to_all(fourier_in, "wave", split_axis=3, concat_axis=0, tiled=True),
        inverse_table,
        preferred_element_type=jnp.float32,
    )
    lat_rows = grid_fields.shape[1]
    forced = forcing(grid_fields)
    columns = coarse_columns(grid_fields)
    regimes = routes[:, 0].reshape(1, -1)
    positions = slot_positions(regimes, devices)[0]
    regime_row = regimes[0]
    capacity = 2 * columns.shape[0] // devices
    outgoing = (
        jnp.zeros((devices, capacity, feat_width), jnp.bfloat16)
        .at[regime_row, positions]
        .set(columns)
    )
    arrived = lax.all_to_all(outgoing, "wave", split_axis=0, concat_axis=0, tiled=True)
    answers = network(arrived.reshape(-1, feat_width), w_in[0], w_mid[0], w_out[0]).reshape(
        arrived.shape
    )
    incoming = lax.all_to_all(answers, "wave", split_axis=0, concat_axis=0, tiled=True)
    returned = incoming[regime_row, positions]
    correction = spread_back(returned, lat_rows)
    tendency_grid = (forced + correction).astype(jnp.bfloat16)
    forward_table = fourier_table(wavenums, NLON, False)
    fourier_out = jnp.einsum(
        "fal,qrl->qfra", tendency_grid, forward_table, preferred_element_type=jnp.float32
    ).astype(jnp.bfloat16)
    received = lax.all_to_all(fourier_out, "wave", split_axis=0, concat_axis=3, tiled=True)
    coeffs = received.reshape(pair_count, 2, received.shape[1], 2, received.shape[3])
    result = masked_forward(legendre, coeffs, side_mask)
    spectral_out = result.astype(jnp.bfloat16)
    return spectral_out.reshape(pair_count, degrees, channels)


def cost(flops, moved):
    return pl.CostEstimate(flops=int(flops), bytes_accessed=int(moved), transcendentals=0)


def channel_order(channels):
    source = jnp.arange(channels, dtype=jnp.int32)
    target = source % 2 * (channels // 2) + source // 2
    return (target[:, None] == source[None, :]).astype(jnp.bfloat16)


def inverse_kernel(spans, devices, low_ref, spectral_ref, legendre_ref, order_ref, *rest):
    outs, scratch = rest[:-1], rest[-1]
    step = pl.program_id(0)
    degrees, channels = spectral_ref.shape[1:]
    lat_total = legendre_ref.shape[1]
    rows = 2 * PAIR_STEP
    degree = lax.broadcasted_iota(jnp.int32, (degrees, channels), 0)
    for i in range(PAIR_STEP):
        low = low_ref[step * PAIR_STEP + i]
        ordered = jnp.dot(spectral_ref[i], order_ref[...], preferred_element_type=jnp.float32)
        lower = degree < degrees - 1 - low
        sides = jnp.concatenate(
            [jnp.where(lower, ordered, 0.0), jnp.where(lower, 0.0, ordered)], axis=1
        ).astype(jnp.bfloat16)
        result = jnp.dot(legendre_ref[i], sides, preferred_element_type=jnp.float32)
        for s in range(2):
            for h in range(channels // 128):
                at = s * channels + h * 128
                scratch[h, pl.ds(2 * i + s, lat_total, stride=rows), :] = result[:, at : at + 128]
    per_device = lat_total // devices
    for out, (first, count) in zip(outs, spans):
        for d in range(devices):
            for h in range(channels // 128):
                block = scratch[h, pl.ds((d * per_device + first) * rows, count * rows), :]
                out[d, :, :, h * 128 : (h + 1) * 128] = block.reshape(count, rows, 128).astype(
                    jnp.bfloat16
                )


def inverse_legendre(spectral, legendre, local_low, order, spans, devices):
    pair_count, degrees, channels = spectral.shape
    lat_total = legendre.shape[1]
    rows = 2 * PAIR_STEP
    return pl.pallas_call(
        functools.partial(inverse_kernel, spans, devices),
        grid_spec=pltpu.PrefetchScalarGridSpec(
            num_scalar_prefetch=1,
            grid=(pair_count // PAIR_STEP,),
            in_specs=[
                pl.BlockSpec((PAIR_STEP, degrees, channels), lambda g, low: (g, 0, 0)),
                pl.BlockSpec((PAIR_STEP, lat_total, degrees), lambda g, low: (g, 0, 0)),
                pl.BlockSpec((channels, channels), lambda g, low: (0, 0)),
            ],
            out_specs=[
                pl.BlockSpec((devices, count, rows, channels), lambda g, low: (0, 0, g, 0))
                for _, count in spans
            ],
            scratch_shapes=[pltpu.VMEM((channels // 128, lat_total * rows, 128), jnp.float32)],
        ),
        out_shape=[
            jax.ShapeDtypeStruct((devices, count, 2 * pair_count, channels), jnp.bfloat16)
            for _, count in spans
        ],
        name="inverse_legendre",
        cost_estimate=cost(
            4 * pair_count * degrees * lat_total * channels, 2 * spectral.size * 2 + 2 * legendre.size
        ),
    )(local_low, spectral, legendre, order)


def grid_kernel(coeff_ref, table_ref, forced_ref, columns_ref, pooled):
    devices, lats, slots, channels = coeff_ref.shape
    feat = channels // 2
    rights = []
    for t in range(lats):
        waves = coeff_ref[:, t].astype(jnp.float32).reshape(devices * slots, channels)
        rights.append(
            jnp.concatenate([waves[:, :feat], waves[:, feat:]], axis=0).astype(jnp.bfloat16)
        )
    fields = jnp.dot(
        table_ref[...], jnp.concatenate(rights, axis=1), preferred_element_type=jnp.float32
    )
    total = None
    for t in range(lats):
        one = fields[:, t * feat : (t + 1) * feat]
        forced_ref[t] = one * pltpu.roll(one, feat - feat // 4, 1)
        total = one if total is None else total + one
    pooled[...] = total
    count = columns_ref.shape[0]
    spread = total.shape[0] // count
    mean = pooled[pl.ds(0, count, stride=spread), :]
    for u in range(1, spread):
        mean = mean + pooled[pl.ds(u, count, stride=spread), :]
    columns_ref[...] = (mean * (1.0 / (spread * lats))).astype(jnp.bfloat16)


def to_grid(coeffs, table):
    devices, lats, slots, channels = coeffs.shape
    points = table.shape[0]
    feat = channels // 2
    return pl.pallas_call(
        grid_kernel,
        grid=(lats // 2,),
        in_specs=[
            pl.BlockSpec((devices, 2, slots, channels), lambda i: (0, i, 0, 0)),
            pl.BlockSpec(table.shape, lambda i: (0, 0)),
        ],
        out_specs=[
            pl.BlockSpec((2, points, feat), lambda i: (i, 0, 0)),
            pl.BlockSpec((points // 4, feat), lambda i: (i, 0)),
        ],
        out_shape=[
            jax.ShapeDtypeStruct((lats, points, feat), jnp.float32),
            jax.ShapeDtypeStruct((lats // 2 * (points // 4), feat), jnp.bfloat16),
        ],
        scratch_shapes=[pltpu.VMEM((points, feat), jnp.float32)],
        name="to_grid",
        cost_estimate=cost(2 * coeffs.size * points, 2 * coeffs.size + 2 * table.size),
    )(coeffs, table)


def fourier_kernel(forced_ref, returned_ref, table_ref, out_ref, fine):
    lats, points, feat = forced_ref.shape
    devices, _, slots, _ = out_ref.shape
    coarse = returned_ref[...].astype(jnp.float32)
    count = coarse.shape[0]
    before = pltpu.roll(coarse, 1, 0)
    following = pltpu.roll(coarse, count - 1, 0)
    pieces = [
        0.375 * before + 0.625 * coarse,
        0.125 * before + 0.875 * coarse,
        0.875 * coarse + 0.125 * following,
        0.625 * coarse + 0.375 * following,
    ]
    for u, piece in enumerate(pieces):
        fine[pl.ds(u, count, stride=4), :] = piece
    correction = fine[...]
    right = jnp.concatenate(
        [(forced_ref[t] + correction).astype(jnp.bfloat16) for t in range(lats)], axis=1
    )
    waves = jnp.dot(table_ref[...], right, preferred_element_type=jnp.float32)
    half = devices * slots
    for t in range(lats):
        for r in range(2):
            part = waves[r * half : (r + 1) * half, t * feat : (t + 1) * feat]
            out_ref[:, t, :, r * feat : (r + 1) * feat] = part.reshape(devices, slots, feat).astype(
                jnp.bfloat16
            )


def to_fourier(forced, returned, table, devices):
    lats, points, feat = forced.shape
    slots = table.shape[0] // (2 * devices)
    return pl.pallas_call(
        fourier_kernel,
        grid=(lats // 2,),
        in_specs=[
            pl.BlockSpec((2, points, feat), lambda i: (i, 0, 0)),
            pl.BlockSpec((points // 4, feat), lambda i: (i, 0)),
            pl.BlockSpec(table.shape, lambda i: (0, 0)),
        ],
        out_specs=pl.BlockSpec((devices, 2, slots, 2 * feat), lambda i: (0, i, 0, 0)),
        out_shape=jax.ShapeDtypeStruct((devices, lats, slots, 2 * feat), jnp.bfloat16),
        scratch_shapes=[pltpu.VMEM((points, feat), jnp.float32)],
        name="to_fourier",
        cost_estimate=cost(2 * forced.size * table.shape[0], 4 * forced.size + 2 * table.size),
    )(forced, returned, table)


def forward_kernel(spans, low_ref, legendre_ref, order_ref, *rest):
    coeffs, out_ref, scratch = rest[:-2], rest[-2], rest[-1]
    step = pl.program_id(0)
    _, degrees, channels = out_ref.shape
    lat_total = legendre_ref.shape[1]
    rows = 2 * PAIR_STEP
    devices = coeffs[0].shape[0]
    per_device = lat_total // devices
    for ref, (first, count) in zip(coeffs, spans):
        for d in range(devices):
            block = ref[d].astype(jnp.float32).reshape(count * rows, channels)
            for h in range(channels // 128):
                scratch[h, pl.ds((d * per_device + first) * rows, count * rows), :] = block[
                    :, h * 128 : (h + 1) * 128
                ]
    degree = lax.broadcasted_iota(jnp.int32, (degrees, channels), 0)
    for i in range(PAIR_STEP):
        low = low_ref[step * PAIR_STEP + i]
        sides = []
        for s in range(2):
            side = jnp.concatenate(
                [
                    scratch[h, pl.ds(2 * i + s, lat_total, stride=rows), :]
                    for h in range(channels // 128)
                ],
                axis=1,
            ).astype(jnp.bfloat16)
            sides.append(
                lax.dot_general(
                    side,
                    order_ref[...],
                    (((1,), (1,)), ((), ())),
                    preferred_element_type=jnp.float32,
                ).astype(jnp.bfloat16)
            )
        both = lax.dot_general(
            legendre_ref[i],
            jnp.concatenate(sides, axis=1),
            (((0,), (0,)), ((), ())),
            preferred_element_type=jnp.float32,
        )
        lower = degree < degrees - 1 - low
        out_ref[i] = jnp.where(lower, both[:, :channels], both[:, channels:]).astype(jnp.bfloat16)


def forward_legendre(coeffs, legendre, local_low, order, spans):
    pair_count, lat_total, degrees = legendre.shape
    channels = order.shape[0]
    rows = 2 * PAIR_STEP
    devices = coeffs[0].shape[0]
    return pl.pallas_call(
        functools.partial(forward_kernel, spans),
        grid_spec=pltpu.PrefetchScalarGridSpec(
            num_scalar_prefetch=1,
            grid=(pair_count // PAIR_STEP,),
            in_specs=[
                pl.BlockSpec((PAIR_STEP, lat_total, degrees), lambda g, low: (g, 0, 0)),
                pl.BlockSpec((channels, channels), lambda g, low: (0, 0)),
            ]
            + [
                pl.BlockSpec((devices, count, rows, channels), lambda g, low: (0, 0, g, 0))
                for _, count in spans
            ],
            out_specs=pl.BlockSpec((PAIR_STEP, degrees, channels), lambda g, low: (g, 0, 0)),
            scratch_shapes=[pltpu.VMEM((channels // 128, lat_total * rows, 128), jnp.float32)],
        ),
        out_shape=jax.ShapeDtypeStruct((pair_count, degrees, channels), jnp.bfloat16),
        name="forward_legendre",
        cost_estimate=cost(
            4 * pair_count * degrees * lat_total * channels, 4 * legendre.size
        ),
    )(local_low, legendre, order, *coeffs)


def smooth(values):
    half = 0.5 * values
    return half + half * jnp.tanh(half)


def network_kernel(
    sent_ref, in_ref, mid_ref, out_ref, result_ref, arrived, answers, sends, arrivals, backs, returns
):
    devices = sent_ref.shape[0]
    me = lax.axis_index("wave")
    barrier = pltpu.get_barrier_semaphore()

    def peer(k):
        other = 0
        for bit in range(devices.bit_length() - 1):
            other = other + (me // (1 << bit) + k // (1 << bit)) % 2 * (1 << bit)
        return other

    def outward(k, source, target):
        return pltpu.make_async_remote_copy(
            src_ref=sent_ref.at[target],
            dst_ref=arrived.at[source],
            send_sem=sends.at[k],
            recv_sem=arrivals.at[k],
            device_id={"wave": peer(k)},
            device_id_type=pl.DeviceIdType.MESH,
        )

    def backward(k, source, owner):
        return pltpu.make_async_remote_copy(
            src_ref=answers.at[source],
            dst_ref=result_ref.at[owner],
            send_sem=backs.at[k],
            recv_sem=returns.at[k],
            device_id={"wave": peer(k)},
            device_id_type=pl.DeviceIdType.MESH,
        )

    def answer(rows):
        hidden = smooth(jnp.dot(rows, in_ref[0], preferred_element_type=jnp.float32))
        deeper = smooth(
            jnp.dot(hidden.astype(jnp.bfloat16), mid_ref[0], preferred_element_type=jnp.float32)
        )
        return jnp.dot(
            deeper.astype(jnp.bfloat16), out_ref[0], preferred_element_type=jnp.float32
        ).astype(jnp.bfloat16)

    def greet(k, carry):
        pl.semaphore_signal(
            barrier, inc=1, device_id={"wave": peer(k)}, device_id_type=pl.DeviceIdType.MESH
        )
        return carry

    def send(i, carry):
        k = devices - i
        outward(k, me, peer(k)).start()
        return carry

    def serve(i, carry):
        k = devices - i
        source = peer(k)
        outward(k, source, peer(k)).wait_recv()
        answers[source] = answer(arrived[source])
        backward(k, source, me).start()
        return carry

    def finish(k, carry):
        outward(k, me, peer(k)).wait_send()
        backward(k, peer(k), me).wait_send()
        backward(k, peer(k), peer(k)).wait_recv()
        return carry

    lax.fori_loop(1, devices, greet, 0)
    pl.semaphore_wait(barrier, devices - 1)
    lax.fori_loop(1, devices, send, 0)
    result_ref[me] = answer(sent_ref[me])
    lax.fori_loop(1, devices, serve, 0)
    lax.fori_loop(1, devices, finish, 0)


def run_network(outgoing, w_in, w_mid, w_out):
    devices, slots, feat = outgoing.shape
    return pl.pallas_call(
        network_kernel,
        in_specs=[pl.BlockSpec(memory_space=pltpu.VMEM)] * 4,
        out_specs=pl.BlockSpec(memory_space=pltpu.VMEM),
        out_shape=jax.ShapeDtypeStruct(outgoing.shape, jnp.bfloat16),
        scratch_shapes=[pltpu.VMEM(outgoing.shape, jnp.bfloat16)] * 2
        + [pltpu.SemaphoreType.DMA((devices,))] * 4,
        compiler_params=pltpu.CompilerParams(collective_id=0, has_side_effects=True),
        name="network",
        cost_estimate=cost(
            2 * devices * slots * (w_in.size + w_mid.size + w_out.size),
            4 * outgoing.size + 2 * w_mid.size,
        ),
    )(outgoing, w_in, w_mid, w_out)


def phase_tables(wavenums, points):
    longitude = jnp.arange(points, dtype=jnp.int32)
    turn = jnp.float32(2.0 * math.pi / points)
    angles = (wavenums[:, None] * longitude[None, :] % points).astype(jnp.float32) * turn
    scale = jnp.float32(1.0 / math.sqrt(points))
    forward = jnp.concatenate([scale * jnp.cos(angles), -scale * jnp.sin(angles)], axis=0).astype(
        jnp.bfloat16
    )
    angles = (longitude[:, None] * wavenums[None, :] % points).astype(jnp.float32) * turn
    factor = jnp.where(wavenums == 0, jnp.float32(1.0), jnp.float32(2.0))[None, :]
    inverse = jnp.concatenate([factor * jnp.cos(angles), -factor * jnp.sin(angles)], axis=1).astype(
        jnp.bfloat16
    )
    return inverse, forward


def exchange(values):
    return lax.all_to_all(values, "wave", split_axis=0, concat_axis=0, tiled=True)


def row_spans(lat_rows):
    pairs = lat_rows // 2
    first = max(1, pairs * 9 // 10)
    spans = [(0, 2 * first), (2 * first, 2 * (pairs - first))]
    return [span for span in spans if span[1] > 0]


def on_device_kernels(spectral, legendre, pair_low, routes, w_in, w_mid, w_out):
    pair_count, degrees, channels = spectral.shape
    feat = channels // 2
    lat_total = legendre.shape[2]
    wave_total = degrees - 1
    devices = lax.axis_size("wave")
    lat_rows = lat_total // devices
    spans = row_spans(lat_rows)
    local_low = lax.dynamic_slice_in_dim(pair_low, lax.axis_index("wave") * pair_count, pair_count)
    order = channel_order(channels)
    turned = jnp.swapaxes(legendre, 1, 2)
    sent = inverse_legendre(spectral, turned, local_low, order, spans, devices)
    pair_low, routes, *sent = lax.optimization_barrier((pair_low, routes, *sent))
    arriving = exchange(sent[0])
    inverse_table, forward_table = phase_tables(slot_waves(pair_low, wave_total), NLON)
    regimes = routes[:, 0]
    total_columns = regimes.shape[0]
    positions = slot_positions(regimes.reshape(1, -1), devices)[0]
    capacity = 2 * total_columns // devices
    places = regimes * capacity + positions
    outgoing = jnp.zeros((devices * capacity, feat), jnp.bfloat16)
    forced = []
    width = NLON // 4
    for part, (first, count) in enumerate(spans):
        held = (arriving, sent[part + 1 :], inverse_table, forward_table, places, outgoing)
        arriving, later, inverse_table, forward_table, places, outgoing = lax.optimization_barrier(
            held
        )
        arrived = arriving
        if later:
            sent[part + 1 :] = later
            arriving = exchange(sent[part + 1])
        forced_part, columns = to_grid(arrived, inverse_table)
        forced.append(forced_part)
        at = places[first // 2 * width : (first + count) // 2 * width]
        outgoing = outgoing.at[at].set(columns, unique_indices=True, mode="promise_in_bounds")
    incoming = run_network(outgoing.reshape(devices, capacity, feat), w_in, w_mid, w_out)
    incoming = incoming.reshape(-1, feat)
    received = [None] * len(spans)
    for part in reversed(range(len(spans))):
        first, count = spans[part]
        at = places[first // 2 * width : (first + count) // 2 * width]
        returned = incoming.at[at].get(mode="promise_in_bounds")
        received[part] = exchange(to_fourier(forced[part], returned, forward_table, devices))
    return forward_legendre(received, turned, local_low, order, spans)


def on_device(spectral, legendre, pair_low, routes, w_in, w_mid, w_out):
    devices = lax.axis_size("wave")
    aligned = (
        spectral.shape[0] % PAIR_STEP == 0
        and 2 * spectral.shape[0] % 8 == 0
        and legendre.shape[2] // devices % 2 == 0
        and 2 * routes.shape[0] // devices % 8 == 0
        and devices & (devices - 1) == 0
    )
    body = on_device_kernels if aligned else on_device_arrays
    return body(spectral, legendre, pair_low, routes, w_in, w_mid, w_out)


def solution(mesh):
    placed = (
        P(("grp", "wave"), None, None),
        P("wave", None, None),
        P(),
        P(("grp", "wave"), None),
        P("wave", None, None),
        P("wave", None, None),
        P("wave", None, None),
    )
    return jax.shard_map(
        on_device,
        mesh=mesh,
        in_specs=placed,
        out_specs=P(("grp", "wave"), None, None),
        check_vma=False,
    )
```
